32 devices in a mesh: groups: 2 (over x), slab: 16 (over z, y, core).
Axes of the slice: x: 2, y: 2, z: 4, core: 2. Of those that a mesh axis runs over, the one named last changes fastest.
Arguments:
- melt_speeds: float32 [3, 64, 32, 512], P(None, ('groups', 'slab')), parts along dimension 1, may hold values from -3 to 3
- heat_state: float32 [64, 32, 512], P(('groups', 'slab')), parts along dimension 0, may hold values from -4 to 4
- eddy_quantities: float32 [2, 64, 32, 512], P(None, ('groups', 'slab')), parts along dimension 1, may hold values from 0.02 to 1
- zone_labels: int32 [32, 16, 256], P(('groups', 'slab')), parts along dimension 0, may hold values from 0 to 7
- zone_resistivity_inverse: float32 [8], replicated, may hold values from 0.05 to 0.4
- imposed_induction: float32 [3, 512, 16, 16], P(None, ('groups', 'slab')), parts along dimension 1, may hold values from -4 to 4
- winding_current: float32 [3, 512, 16, 16], P(None, ('groups', 'slab')), parts along dimension 1, may hold values from -4 to 4
- window_entry_induction_guess: float32 [3, 512, 16, 16], P(None, ('groups', 'slab')), parts along dimension 1, may hold values from 1 to 4
Outputs:
- velocity_out: float32 [3, 64, 32, 512], P(None, ('groups', 'slab')), parts along dimension 1
- temperature_out: float32 [64, 32, 512], P(('groups', 'slab')), parts along dimension 0
- turbulence_out: float32 [2, 64, 32, 512], P(None, ('groups', 'slab')), parts along dimension 1
- potential: float32 [3, 512, 16, 16], P(None, ('groups', 'slab')), parts along dimension 1
The draws below stay inside these ranges and needn't reach their ends.
There are 2 independent parts, one for each index of `groups`. The reference program is written for one: setup_inputs(seed, part) draws one part's arguments, and reference() takes and returns one part's arrays. A program takes and returns all parts, laid end to end along the dimension named above; an argument that names none is the same for every part. Nothing has to cross between parts.
Inputs may be any that keep to these rules, and one draw needn't show every extreme that they name: `zone_labels`: region number of each coarse block.
All inputs are finite; a program needn't handle non-finite values.
Results may differ from the reference program's by a relative error of at most 0.0001.
Values sent between devices are 32-bit elements; how exact they have to be, the bound alone decides.
No kernel may reach another device: no remote copies, remote signals or barrier semaphores. Data moves between devices by JAX's collectives and lax.ppermute only.
A program may use at most 128 MiB of HBM per device.

```python
import math
import jax
import jax.numpy as jnp

NARROW_BINS_NORTH = 32
NARROW_BINS_EAST = 512
STEPS = 2
SWEEPS = 8
REGIONS = 8
NARROW_BINS_HIGH = 32
XH = 256
YH = 16
ZH = 16


def draw_window_entry_induction_guess(key, part):
    phase_key = jax.random.fold_in(key, 71)
    rough_key = jax.random.fold_in(key, 72)
    phase = jax.random.uniform(phase_key, (3, 1, 1, 1), jnp.float32, 0.0, 2.0 * math.pi)
    depth = jnp.arange(ZH, dtype=jnp.float32)[None, None, None, :]
    wave = jnp.cos(4.0 * math.pi * depth / ZH + phase)
    rough = jnp.clip(0.4 * jax.random.normal(rough_key, (3, XH, YH, ZH), jnp.float32), -0.8, 0.8)
    return (2.5 + 0.6 * wave + rough).astype(jnp.float32)


def set_ends(entries, rng, smallest, high):
    longest = entries.shape.index(max(entries.shape))
    spots = []
    for shift in (0, 1):
        where = [jax.random.randint(jax.random.fold_in(rng, axis), (), 0, length) for axis, length in enumerate(entries.shape)]
        where[longest] = (where[longest] + shift) % entries.shape[longest]
        spots.append(tuple(where))
    return entries.at[spots[0]].set(smallest).at[spots[1]].set(high)


def shard_levels(key, shape, shards, low, high):
    def one(dim, shards_of):
        heights = jax.random.uniform(jax.random.fold_in(jax.random.fold_in(key, 6), dim), (shards_of,), jnp.float32, low / len(shards), high / len(shards))
        return jnp.repeat(jnp.exp(heights), shape[dim] // shards_of).reshape((-1,) + (1,) * (len(shape) - dim - 1))

    level = one(*shards[0])
    for cut in shards[1:]:
        level = level * one(*cut)
    return level


def gaussian(key, dims, scale, limit, shards=(), kind=jnp.bfloat16):
    array = scale * jax.random.normal(key, dims, jnp.float32)
    if shards:
        array = array * shard_levels(key, dims, shards, -0.22, 0.18)
    return jnp.clip(array, -limit, limit).astype(kind)


def setup_inputs(seed: int = 0, part: int = 0) -> dict:
    seeds = jax.random.split(jax.random.key(seed), 9)
    part_splits = jax.random.split(jax.random.fold_in(seeds[8], part), 9)
    return {
        "melt_speeds": gaussian(part_splits[0], (3, NARROW_BINS_HIGH, NARROW_BINS_NORTH, NARROW_BINS_EAST), 0.5, 3.0, ((1, 16),), jnp.float32),
        "heat_state": gaussian(part_splits[1], (NARROW_BINS_HIGH, NARROW_BINS_NORTH, NARROW_BINS_EAST), 1.0, 4.0, ((0, 16),), jnp.float32),
        "eddy_quantities": jnp.clip(jnp.exp(math.log(1.0) - 3.912023 * jax.random.uniform(part_splits[2], (2, NARROW_BINS_HIGH, NARROW_BINS_NORTH, NARROW_BINS_EAST), jnp.float32) ** shard_levels(part_splits[2], (2, NARROW_BINS_HIGH, NARROW_BINS_NORTH, NARROW_BINS_EAST), ((1, 16),), -0.2, 0.2)), 0.02, 1.0),
        "zone_labels": set_ends(jax.random.randint(part_splits[3], (ZH, YH, XH), 0, REGIONS), jax.random.fold_in(part_splits[3], 1), 0, REGIONS - 1).astype(jnp.int32),
        "zone_resistivity_inverse": jnp.clip(jnp.exp(jax.random.uniform(seeds[4], (REGIONS,), jnp.float32, math.log(0.05), math.log(0.4))), 0.05, 0.4),
        "imposed_induction": gaussian(part_splits[5], (3, XH, YH, ZH), 1.0, 4.0, ((1, 16),), jnp.float32),
        "winding_current": gaussian(part_splits[6], (3, XH, YH, ZH), 1.0, 4.0, ((1, 16),), jnp.float32),
        "window_entry_induction_guess": draw_window_entry_induction_guess(jax.random.fold_in(jax.random.fold_in(seeds[8], part), 71), part),
    }


time_step = 0.02
molecular = 0.01
heat_diffuse = 0.01
eddy_coeff = 0.09
prod_coeff = 1.44
dissip_coeff = 1.92
turb_floor = 0.05
coupling = 1.0
thermal_gradient_factor = 0.3


def reduce_onto_parent(block):
    comps, depth, rows, cols = block.shape
    shaped = block.reshape(comps, depth // 2, 2, rows // 2, 2, cols // 2, 2)
    return jnp.mean(shaped, axis=(2, 4, 6))


def prolong(block):
    comps, depth, rows, cols = block.shape
    wide = jnp.broadcast_to(block[:, :, None, :, None, :, None], (comps, depth, 2, rows, 2, cols, 2))
    return wide.reshape(comps, depth * 2, rows * 2, cols * 2)


def cross(left_vec, right_vec):
    return jnp.stack([left_vec[1] * right_vec[2] - left_vec[2] * right_vec[1],
                      left_vec[2] * right_vec[0] - left_vec[0] * right_vec[2],
                      left_vec[0] * right_vec[1] - left_vec[1] * right_vec[0]], 0)


def neighbours(padded):
    return (padded[:, 2:, 1:-1, 1:-1] + padded[:, :-2, 1:-1, 1:-1] + padded[:, 1:-1, 2:, 1:-1]
            + padded[:, 1:-1, :-2, 1:-1] + padded[:, 1:-1, 1:-1, 2:] + padded[:, 1:-1, 1:-1, :-2])


def ohmic_admittance(zone_labels, zone_resistivity_inverse, heat_state):
    labels = jnp.arange(zone_resistivity_inverse.shape[0], dtype=jnp.int32)
    onehot = zone_labels[None] == labels[:, None, None, None]
    searched_higher = jnp.sum(jnp.where(onehot, zone_resistivity_inverse[:, None, None, None], jnp.float32(0.0)), axis=0)
    return searched_higher * reduce_onto_parent(jnp.exp(-thermal_gradient_factor * heat_state)[None])[0]


def relax(coupled, imposed_induction, winding_current, potential, face_fn):
    conduct = coupled[3]
    motional = cross(coupled[:3], imposed_induction)
    source = conduct * motional + winding_current
    diagonal = 6.0 + coupling * conduct
    for sweep_index in range(SWEEPS):
        potential = (source + neighbours(face_fn(potential))) / diagonal
    drive_field = motional - coupling * potential
    current = conduct * drive_field + winding_current
    lorentz = cross(current, imposed_induction)
    joule = conduct * jnp.sum(drive_field * drive_field, axis=0)
    return potential, jnp.concatenate([lorentz, joule[None]], 0)


def advance(padded, lorentz, joule):
    bordered = jnp.pad(padded, ((0, 0), (0, 0), (0, 0), (1, 1)))
    center = bordered[:, 1:-1, 1:-1, 1:-1]
    z_plus = bordered[:, 2:, 1:-1, 1:-1]
    z_minus = bordered[:, :-2, 1:-1, 1:-1]
    y_plus = bordered[:, 1:-1, 2:, 1:-1]
    y_minus = bordered[:, 1:-1, :-2, 1:-1]
    x_plus = bordered[:, 1:-1, 1:-1, 2:]
    x_minus = bordered[:, 1:-1, 1:-1, :-2]
    grad_z = 0.5 * (z_plus - z_minus)
    grad_y = 0.5 * (y_plus - y_minus)
    grad_x = 0.5 * (x_plus - x_minus)
    laplace = z_plus + z_minus + y_plus + y_minus + x_plus + x_minus - 6.0 * center
    kinetic = center[4]
    dissip = center[5]
    transport = center[0] * grad_x + center[1] * grad_y + center[2] * grad_z
    eddy_visc = eddy_coeff * kinetic * kinetic / jnp.maximum(dissip, turb_floor)
    strain = jnp.sum(grad_x[:3] * grad_x[:3] + grad_y[:3] * grad_y[:3] + grad_z[:3] * grad_z[:3], axis=0)
    produce = eddy_visc * strain
    diffuse = jnp.stack([molecular + eddy_visc, molecular + eddy_visc, molecular + eddy_visc,
                         heat_diffuse + eddy_visc / 0.9, molecular + eddy_visc, molecular + eddy_visc / 1.3], 0)
    dissip_source = (prod_coeff * produce - dissip_coeff * dissip) * dissip / jnp.maximum(kinetic, turb_floor)
    source = jnp.concatenate([lorentz, joule[None], (produce - dissip)[None], dissip_source[None]], 0)
    return center + time_step * (diffuse * laplace - transport + source)


def pad_all(potential):
    return jnp.pad(potential, ((0, 0), (1, 1), (1, 1), (1, 1)))


def reference(melt_speeds, heat_state, eddy_quantities, zone_labels, zone_resistivity_inverse, imposed_induction, winding_current, window_entry_induction_guess):
    induction_tables = jnp.concatenate([melt_speeds, heat_state[None], eddy_quantities], 0)
    potential = window_entry_induction_guess
    for step_index in range(STEPS):
        conduct = ohmic_admittance(zone_labels, zone_resistivity_inverse, induction_tables[3])
        coupled = jnp.concatenate([reduce_onto_parent(induction_tables[:3]), conduct[None]], 0)
        coupled = jnp.transpose(coupled, (0, 3, 2, 1))
        potential, em_loads = relax(coupled, imposed_induction, winding_current, potential, pad_all)
        em_loads = prolong(jnp.transpose(em_loads, (0, 3, 2, 1)))
        padded = jnp.pad(induction_tables, ((0, 0), (1, 1), (1, 1), (0, 0)))
        induction_tables = advance(padded, em_loads[:3], em_loads[3])
    return induction_tables[:3], induction_tables[3], induction_tables[4:], potential
```

```python
import functools

import jax
import jax.numpy as jnp
from jax import lax
from jax.experimental import pallas as pl
from jax.experimental.pallas import tpu as pltpu
from jax.sharding import PartitionSpec as P

STEPS = 2
SWEEPS = 8


time_step = 0.02
molecular = 0.01
heat_diffuse = 0.01
eddy_coeff = 0.09
prod_coeff = 1.44
dissip_coeff = 1.92
turb_floor = 0.05
coupling = 1.0
thermal_gradient_factor = 0.3


def extended(block, sides, width):
    for axis, dim in sides:
        count = lax.axis_size(axis)
        forward = [(i, i + 1) for i in range(count - 1)]
        backward = [(target, source) for source, target in forward]
        low = lax.ppermute(
            lax.slice_in_dim(block, block.shape[dim] - width, None, axis=dim), axis, forward
        )
        high = lax.ppermute(lax.slice_in_dim(block, 0, width, axis=dim), axis, backward)
        block = jnp.concatenate([low, block, high], axis=dim)
    return block


def reduce_onto_parent(block):
    comps, depth, rows, cols = block.shape
    shaped = block.reshape(comps, depth // 2, 2, rows // 2, 2, cols // 2, 2)
    return jnp.mean(shaped, axis=(2, 4, 6))


def prolong(block):
    comps, depth, rows, cols = block.shape
    wide = jnp.broadcast_to(
        block[:, :, None, :, None, :, None], (comps, depth, 2, rows, 2, cols, 2)
    )
    return wide.reshape(comps, depth * 2, rows * 2, cols * 2)


def cross(left_vec, right_vec):
    return jnp.stack(
        [
            left_vec[1] * right_vec[2] - left_vec[2] * right_vec[1],
            left_vec[2] * right_vec[0] - left_vec[0] * right_vec[2],
            left_vec[0] * right_vec[1] - left_vec[1] * right_vec[0],
        ],
        0,
    )


def neighbours(padded):
    return (
        padded[:, 2:, 1:-1, 1:-1]
        + padded[:, :-2, 1:-1, 1:-1]
        + padded[:, 1:-1, 2:, 1:-1]
        + padded[:, 1:-1, :-2, 1:-1]
        + padded[:, 1:-1, 1:-1, 2:]
        + padded[:, 1:-1, 1:-1, :-2]
    )


def ohmic_admittance(zone_labels, zone_resistivity_inverse, heat_state):
    labels = jnp.arange(zone_resistivity_inverse.shape[0], dtype=jnp.int32)
    onehot = zone_labels[None] == labels[:, None, None, None]
    searched_higher = jnp.sum(
        jnp.where(onehot, zone_resistivity_inverse[:, None, None, None], jnp.float32(0.0)), axis=0
    )
    return (
        searched_higher
        * reduce_onto_parent(jnp.exp(-thermal_gradient_factor * heat_state)[None])[0]
    )


def faces(potential):
    padded = extended(potential, (("slab", 1),), 1)
    return jnp.pad(padded, ((0, 0), (0, 0), (1, 1), (1, 1)))


def relax(coupled, imposed_induction, winding_current, potential):
    conduct = coupled[3]
    motional = cross(coupled[:3], imposed_induction)
    source = conduct * motional + winding_current
    diagonal = 6.0 + coupling * conduct
    for sweep_index in range(SWEEPS):
        potential = (source + neighbours(faces(potential))) / diagonal
    drive_field = motional - coupling * potential
    current = conduct * drive_field + winding_current
    lorentz = cross(current, imposed_induction)
    joule = conduct * jnp.sum(drive_field * drive_field, axis=0)
    return (potential, jnp.concatenate([lorentz, joule[None]], 0))


def advance(padded, lorentz, joule):
    bordered = jnp.pad(padded, ((0, 0), (0, 0), (0, 0), (1, 1)))
    center = bordered[:, 1:-1, 1:-1, 1:-1]
    z_plus = bordered[:, 2:, 1:-1, 1:-1]
    z_minus = bordered[:, :-2, 1:-1, 1:-1]
    y_plus = bordered[:, 1:-1, 2:, 1:-1]
    y_minus = bordered[:, 1:-1, :-2, 1:-1]
    x_plus = bordered[:, 1:-1, 1:-1, 2:]
    x_minus = bordered[:, 1:-1, 1:-1, :-2]
    grad_z = 0.5 * (z_plus - z_minus)
    grad_y = 0.5 * (y_plus - y_minus)
    grad_x = 0.5 * (x_plus - x_minus)
    laplace = z_plus + z_minus + y_plus + y_minus + x_plus + x_minus - 6.0 * center
    kinetic = center[4]
    dissip = center[5]
    transport = center[0] * grad_x + center[1] * grad_y + center[2] * grad_z
    eddy_visc = eddy_coeff * kinetic * kinetic / jnp.maximum(dissip, turb_floor)
    strain = jnp.sum(
        grad_x[:3] * grad_x[:3] + grad_y[:3] * grad_y[:3] + grad_z[:3] * grad_z[:3], axis=0
    )
    produce = eddy_visc * strain
    diffuse = jnp.stack(
        [
            molecular + eddy_visc,
            molecular + eddy_visc,
            molecular + eddy_visc,
            heat_diffuse + eddy_visc / 0.9,
            molecular + eddy_visc,
            molecular + eddy_visc / 1.3,
        ],
        0,
    )
    dissip_source = (
        (prod_coeff * produce - dissip_coeff * dissip) * dissip / jnp.maximum(kinetic, turb_floor)
    )
    source = jnp.concatenate(
        [lorentz, joule[None], (produce - dissip)[None], dissip_source[None]], 0
    )
    return center + time_step * (diffuse * laplace - transport + source)


def flow_step(induction_tables, em_loads):
    padded = extended(induction_tables, (("slab", 1),), 1)
    padded = jnp.pad(padded, ((0, 0), (0, 0), (1, 1), (0, 0)))
    return advance(padded, em_loads[:3], em_loads[3])


def local_coupled(induction_tables, zone_labels, zone_resistivity_inverse):
    conduct = ohmic_admittance(zone_labels, zone_resistivity_inverse, induction_tables[3])
    return jnp.concatenate([reduce_onto_parent(induction_tables[:3]), conduct[None]], 0)


def per_sweep_plan(
    melt_speeds,
    heat_state,
    eddy_quantities,
    zone_labels,
    zone_resistivity_inverse,
    imposed_induction,
    winding_current,
    window_entry_induction_guess,
):
    induction_tables = jnp.concatenate([melt_speeds, heat_state[None], eddy_quantities], 0)
    arrived = (
        lax.all_to_all(
            window_entry_induction_guess, "slab", split_axis=3, concat_axis=1, tiled=True
        ),
        lax.all_to_all(imposed_induction, "slab", split_axis=3, concat_axis=1, tiled=True),
        lax.all_to_all(winding_current, "slab", split_axis=3, concat_axis=1, tiled=True),
    )
    potential = jnp.transpose(arrived[0], (0, 3, 2, 1))
    field_local = jnp.transpose(arrived[1], (0, 3, 2, 1))
    coil_local = jnp.transpose(arrived[2], (0, 3, 2, 1))
    for step_index in range(STEPS):
        coupled = local_coupled(induction_tables, zone_labels, zone_resistivity_inverse)
        potential, em_loads = relax(coupled, field_local, coil_local, potential)
        induction_tables = flow_step(induction_tables, prolong(em_loads))
    potential = lax.all_to_all(
        jnp.transpose(potential, (0, 3, 2, 1)), "slab", split_axis=1, concat_axis=3, tiled=True
    )
    return (induction_tables[:3], induction_tables[3], induction_tables[4:], potential)


HALO = 2 * SWEEPS
LANES = 128


def exact_dot(values, chooser):
    high = values.astype(jnp.bfloat16)
    rest = values - high.astype(jnp.float32)
    middle = rest.astype(jnp.bfloat16)
    low = (rest - middle.astype(jnp.float32)).astype(jnp.bfloat16)
    rows = values.shape[0]
    parts = jnp.dot(
        jnp.concatenate([high, middle, low], 0), chooser, preferred_element_type=jnp.float32
    )
    return parts[:rows] + (parts[rows : 2 * rows] + parts[2 * rows :])


def pair_chooser(wide, weight, transposed):
    shape = (wide // 2, wide) if transposed else (wide, wide // 2)
    fine = lax.broadcasted_iota(jnp.int32, shape, 1 if transposed else 0)
    coarse = lax.broadcasted_iota(jnp.int32, shape, 0 if transposed else 1)
    picked = lax.shift_right_logical(fine, 1) == coarse
    return jnp.where(picked, jnp.float32(weight), jnp.float32(0.0)).astype(jnp.bfloat16)


def pack_windows(sums_ref, labels_ref, table_ref, send_ref, halo):
    tiles, rows, _ = sums_ref.shape
    wide = tiles * LANES
    count, ny = send_ref.shape[0], labels_ref.shape[1]
    paired = jnp.concatenate(
        [
            sums_ref[t, pl.ds(0, rows // 2, stride=2), :] + sums_ref[t, pl.ds(1, rows // 2, stride=2), :]
            for t in range(tiles)
        ],
        1,
    )
    coarse = exact_dot(paired, pair_chooser(wide, 0.125, False))
    labels = labels_ref[0]
    admittance = jnp.zeros(labels.shape, jnp.float32)
    for region in range(table_ref.shape[0]):
        admittance = jnp.where(labels == region, table_ref[region], admittance)
    coupled = jnp.concatenate([coarse[: 3 * ny], coarse[3 * ny :] * admittance], 0)
    nx = wide // 2
    chunk = nx // count
    window = chunk + 2 * halo
    padded = jnp.concatenate([coupled, jnp.zeros((4 * ny, LANES), jnp.float32)], 1)
    padded = pltpu.roll(padded, halo, 1)
    for target in range(count):
        start = target * chunk
        joined = jnp.concatenate(
            [padded[f * ny : (f + 1) * ny, start : start + window] for f in range(4)], 1
        )
        send_ref[target, :ny, :] = joined[:, :LANES]
        if 4 * window > LANES:
            half = ny // 2
            send_ref[target, ny:, :] = jnp.concatenate(
                [joined[:half, LANES:], joined[half:, LANES:]], 1
            )


def open_kernel(
    vel_ref,
    heat_ref,
    turb_ref,
    labels_ref,
    table_ref,
    guess_ref,
    applied_ref,
    coil_ref,
    send_ref,
    block_ref,
    mate_ref,
    cross_ref,
    sums_ref,
    flat_ref,
):
    odd = lax.rem(lax.axis_index("slab"), 2)
    planes = [(vel_ref, 0), (vel_ref, 1), (vel_ref, 2), (heat_ref, None), (turb_ref, 0), (turb_ref, 1)]
    for f, (ref, comp) in enumerate(planes):
        if comp is None:
            mate_ref[f] = ref[1 - odd]
            cross_ref[f] = ref[odd]
        else:
            mate_ref[f] = ref[comp, 1 - odd]
            cross_ref[f] = ref[comp, odd]
    rows = heat_ref.shape[1]
    for t in range(sums_ref.shape[0]):
        at = slice(t * LANES, (t + 1) * LANES)
        for c in range(3):
            sums_ref[t, c * rows : (c + 1) * rows, :] = vel_ref[c, 0, :, at] + vel_ref[c, 1, :, at]
        sums_ref[t, 3 * rows :, :] = jnp.exp(
            -thermal_gradient_factor * heat_ref[0, :, at]
        ) + jnp.exp(-thermal_gradient_factor * heat_ref[1, :, at])
    total, nz = guess_ref.shape
    ny = labels_ref.shape[1]
    stacked = total // ny
    for kind, ref in enumerate((guess_ref, applied_ref, coil_ref)):
        flat_ref[:, kind * nz : (kind + 1) * nz] = ref[...]
    lines = [flat_ref[pl.ds(y, stacked, stride=ny), :] for y in range(ny)]
    for kind in range(3):
        block_ref[kind * stacked : (kind + 1) * stacked, :] = jnp.concatenate(
            [line[:, kind * nz : (kind + 1) * nz] for line in lines], 1
        )
    pack_windows(sums_ref, labels_ref, table_ref, send_ref, HALO)


def solve_kernel(chunk, ny, nz, first, *refs):
    if first:
        recv_ref, block_ref, mate_ref, cross_ref, pot_out, send_ref, wide_ref, turn_ref = refs
        halo = HALO
    else:
        recv_ref, block_ref, mate_ref, cross_ref, pot_in, pot_out, send_ref = refs[:7]
        wide_ref, turn_ref, flat_ref = refs[7:]
        halo = HALO - SWEEPS
    window = chunk + 2 * halo
    place = lax.axis_index("slab")
    count = lax.axis_size("slab")
    odd = lax.rem(place, 2)
    half = ny // 2
    for z in range(nz):
        wide_ref[0, pl.ds(z, ny, stride=nz), :] = recv_ref[z, :ny, :]
        if 4 * window > LANES:
            tail = recv_ref[z, ny:, :]
            wide_ref[1, pl.ds(z, half, stride=nz), :] = tail
            wide_ref[1, pl.ds(half * nz + z, half, stride=nz), :] = pltpu.roll(tail, LANES // 2, 1)
    turned = jnp.concatenate([jnp.transpose(wide_ref[t]) for t in range(wide_ref.shape[0])], 0)
    velocity = [turned[c * window : (c + 1) * window] for c in range(3)]
    conduct = turned[3 * window : 4 * window]

    def windowed(kind):
        found = []
        for c in range(3):
            base = (kind * 3 + c) * chunk
            mate, cross_side = mate_ref[base : base + chunk, :], cross_ref[base : base + chunk, :]
            low = jnp.where(odd == 0, cross_side, mate)
            high = jnp.where(odd == 0, mate, cross_side)
            found.append(
                jnp.concatenate(
                    [low[chunk - halo :], block_ref[base : base + chunk, :], high[:halo]], 0
                )
            )
        return found

    applied, coil = windowed(1), windowed(2)
    potential = jnp.concatenate(windowed(0), 0) if first else pot_in[...]
    motional = [
        velocity[1] * applied[2] - velocity[2] * applied[1],
        velocity[2] * applied[0] - velocity[0] * applied[2],
        velocity[0] * applied[1] - velocity[1] * applied[0],
    ]
    where_x = place * chunk - halo + lax.broadcasted_iota(jnp.int32, (window, ny * nz), 0)
    inside = (where_x >= 0) & (where_x < count * chunk)
    inverse = jnp.where(inside, 1.0 / (6.0 + coupling * conduct), 0.0)
    source = jnp.concatenate([conduct * motional[c] + coil[c] for c in range(3)], 0)
    inverse = jnp.concatenate([inverse] * 3, 0)
    source = source * inverse
    shape = potential.shape
    lane = lax.broadcasted_iota(jnp.int32, shape, 1)
    column = lax.rem(lane, nz)
    for sweep in range(SWEEPS):
        around = pltpu.roll(potential, 1, 0) + pltpu.roll(potential, shape[0] - 1, 0)
        around += jnp.where(column == 0, 0.0, pltpu.roll(potential, 1, 1))
        around += jnp.where(column == nz - 1, 0.0, pltpu.roll(potential, shape[1] - 1, 1))
        around += jnp.where(lane < nz, 0.0, pltpu.roll(potential, nz, 1))
        around += jnp.where(lane >= shape[1] - nz, 0.0, pltpu.roll(potential, shape[1] - nz, 1))
        potential = source + around * inverse
    own = [potential[c * window + halo : c * window + halo + chunk] for c in range(3)]
    if first:
        keep = chunk + 2 * (halo - SWEEPS)
        for c in range(3):
            pot_out[c * keep : (c + 1) * keep, :] = potential[
                c * window + SWEEPS : c * window + SWEEPS + keep
            ]
    else:
        together = jnp.concatenate(own, 0)
        lanes = ny * nz
        for y in range(ny):
            line = pltpu.roll(together, lanes - y * nz, 1) if y else together
            flat_ref[pl.ds(y, 3 * chunk, stride=ny), :] = line[:, :LANES]
        pot_out[...] = flat_ref[:, :nz]
    mine = slice(halo, halo + chunk)
    conduct_own = conduct[mine]
    applied_own = [a[mine] for a in applied]
    drive = [motional[c][mine] - coupling * own[c] for c in range(3)]
    current = [conduct_own * drive[c] + coil[c][mine] for c in range(3)]
    loads = [
        current[1] * applied_own[2] - current[2] * applied_own[1],
        current[2] * applied_own[0] - current[0] * applied_own[2],
        current[0] * applied_own[1] - current[1] * applied_own[0],
        conduct_own * (drive[0] * drive[0] + drive[1] * drive[1] + drive[2] * drive[2]),
    ]
    loads = jnp.concatenate(loads, 0)
    middle = half * nz
    turn_ref[...] = jnp.transpose(jnp.concatenate([loads[:, :middle], loads[:, middle:]], 0))
    for z in range(nz):
        send_ref[z] = turn_ref[pl.ds(z, half, stride=nz), :]


def flow_kernel(last, *refs):
    vel_ref, heat_ref, turb_ref, mate_ref, cross_ref, recv_ref = refs[:6]
    if last:
        vel_out, heat_out, turb_out, bordered_ref, loads_ref = refs[6:]
    else:
        labels_ref, table_ref = refs[6:8]
        vel_out, heat_out, turb_out, send_ref, mate_out, cross_out = refs[8:14]
        bordered_ref, loads_ref, sums_ref = refs[14:]
    odd = lax.rem(lax.axis_index("slab"), 2)
    rows, wide = heat_ref.shape[1:]
    count, half, packed = recv_ref.shape
    chunk = packed // 8
    edge = jnp.zeros((8, wide), jnp.float32)
    for f in range(6):
        for plane in range(2):
            bordered_ref[f, plane, 0:8, :] = edge
            bordered_ref[f, plane, 8 + rows :, :] = edge
            if f < 3:
                block = vel_ref[f, plane]
            elif f == 3:
                block = heat_ref[plane]
            else:
                block = turb_ref[f - 4, plane]
            bordered_ref[f, plane, 8 : 8 + rows, :] = block
    stacked = []
    for f in range(4):
        for side in range(2):
            at = (side * 4 + f) * chunk
            stacked.append(
                jnp.concatenate([recv_ref[s, :, at : at + chunk] for s in range(count)], 1)
            )
    spread = exact_dot(jnp.concatenate(stacked, 0), pair_chooser(wide, 1.0, True))
    for t in range(wide // LANES):
        part = spread[:, t * LANES : (t + 1) * LANES]
        loads_ref[t, pl.ds(0, 2 * rows, stride=2), :] = part
        loads_ref[t, pl.ds(1, 2 * rows, stride=2), :] = part
    lane = lax.broadcasted_iota(jnp.int32, (8, wide), 1)
    first_lane, last_lane = lane == 0, lane == wide - 1
    for top in range(0, rows, 8):
        tile = slice(top, top + 8)
        for plane in range(2):
            center = [bordered_ref[f, plane, 8 + top : 16 + top, :] for f in range(6)]
            kinetic, dissip = center[4], center[5]
            eddy_visc = eddy_coeff * kinetic * kinetic / jnp.maximum(dissip, turb_floor)
            strain = jnp.zeros((8, wide), jnp.float32)
            for f in range(6):
                here = center[f]
                mate, cross_side = mate_ref[f, tile, :], cross_ref[f, tile, :]
                other = bordered_ref[f, 1 - plane, 8 + top : 16 + top, :]
                if plane == 0:
                    z_minus, z_plus = jnp.where(odd == 0, cross_side, mate), other
                else:
                    z_minus, z_plus = other, jnp.where(odd == 0, mate, cross_side)
                y_minus = bordered_ref[f, plane, 7 + top : 15 + top, :]
                y_plus = bordered_ref[f, plane, 9 + top : 17 + top, :]
                x_minus = jnp.where(first_lane, 0.0, pltpu.roll(here, 1, 1))
                x_plus = jnp.where(last_lane, 0.0, pltpu.roll(here, wide - 1, 1))
                grad_z = 0.5 * (z_plus - z_minus)
                grad_y = 0.5 * (y_plus - y_minus)
                grad_x = 0.5 * (x_plus - x_minus)
                laplace = z_plus + z_minus + y_plus + y_minus + x_plus + x_minus - 6.0 * here
                transport = center[0] * grad_x + center[1] * grad_y + center[2] * grad_z
                if f < 3:
                    strain += grad_x * grad_x + grad_y * grad_y + grad_z * grad_z
                    diffuse = molecular + eddy_visc
                    source = jnp.concatenate(
                        [
                            loads_ref[t, f * rows + top : f * rows + top + 8, :]
                            for t in range(wide // LANES)
                        ],
                        1,
                    )
                elif f == 3:
                    diffuse = heat_diffuse + eddy_visc * (1.0 / 0.9)
                    source = jnp.concatenate(
                        [
                            loads_ref[t, f * rows + top : f * rows + top + 8, :]
                            for t in range(wide // LANES)
                        ],
                        1,
                    )
                elif f == 4:
                    produce = eddy_visc * strain
                    diffuse = molecular + eddy_visc
                    source = produce - dissip
                else:
                    diffuse = molecular + eddy_visc * (1.0 / 1.3)
                    source = (
                        (prod_coeff * produce - dissip_coeff * dissip)
                        * dissip
                        / jnp.maximum(kinetic, turb_floor)
                    )
                fresh = here + time_step * (diffuse * laplace - transport + source)
                if f < 3:
                    vel_out[f, plane, tile, :] = fresh
                elif f == 3:
                    heat_out[plane, tile, :] = fresh
                else:
                    turb_out[f - 4, plane, tile, :] = fresh
                if not last and f < 4:
                    part = jnp.exp(-thermal_gradient_factor * fresh) if f == 3 else fresh
                    spot = slice(f * rows + top, f * rows + top + 8)
                    for t in range(wide // LANES):
                        piece = part[:, t * LANES : (t + 1) * LANES]
                        sums_ref[t, spot, :] = piece if plane == 0 else sums_ref[t, spot, :] + piece
    if last:
        return
    outs = [(vel_out, 0), (vel_out, 1), (vel_out, 2), (heat_out, None), (turb_out, 0), (turb_out, 1)]
    for f, (ref, comp) in enumerate(outs):
        if comp is None:
            mate_out[f] = ref[1 - odd]
            cross_out[f] = ref[odd]
        else:
            mate_out[f] = ref[comp, 1 - odd]
            cross_out[f] = ref[comp, odd]
    pack_windows(sums_ref, labels_ref, table_ref, send_ref, HALO - SWEEPS)


def call(kernel, outs, scratch, name, table_at, cost, *operands):
    vmem = pl.BlockSpec(memory_space=pltpu.VMEM)
    smem = pl.BlockSpec(memory_space=pltpu.SMEM)
    return pl.pallas_call(
        kernel,
        out_shape=[jax.ShapeDtypeStruct(s, jnp.float32) for s in outs],
        in_specs=[smem if i == table_at else vmem for i in range(len(operands))],
        out_specs=[vmem] * len(outs),
        scratch_shapes=[pltpu.VMEM(s, jnp.float32) for s in scratch],
        name=name,
        cost_estimate=pl.CostEstimate(flops=cost, bytes_accessed=4 * cost // 64, transcendentals=0),
    )(*operands)


def beside(block):
    count = lax.axis_size("slab")
    mates = [(i, i ^ 1) for i in range(count)]
    across = [(i, i + 1) for i in range(1, count - 1, 2)]
    across = across + [(b, a) for a, b in across]
    return mates, across


def window_plan(
    melt_speeds,
    heat_state,
    eddy_quantities,
    zone_labels,
    zone_resistivity_inverse,
    imposed_induction,
    winding_current,
    window_entry_induction_guess,
):
    count = lax.axis_size("slab")
    _, chunk, ny, nz = imposed_induction.shape
    _, rows, wide = heat_state.shape
    mates, across = beside(None)
    flat = [
        a.reshape(3 * chunk * ny, nz)
        for a in (window_entry_induction_guess, imposed_induction, winding_current)
    ]
    window, narrow = chunk + 2 * HALO, chunk + 2 * (HALO - SWEEPS)
    tall = ny + ny // 2 if 4 * window > LANES else ny
    plane = (6, rows, wide)
    sums = (wide // LANES, 4 * rows, LANES)
    fields = (melt_speeds, heat_state, eddy_quantities)
    send, block, mate_plane, cross_plane = call(
        open_kernel,
        [(count, tall, LANES), (9 * chunk, ny * nz), plane, plane],
        [sums, (3 * chunk * ny, LANES)],
        "open_windows",
        4,
        1 << 22,
        *fields,
        zone_labels,
        zone_resistivity_inverse,
        *flat,
    )
    block_mate = lax.ppermute(block, "slab", mates)
    block_cross = lax.ppermute(block, "slab", across)
    halo_mate = lax.ppermute(mate_plane, "slab", mates)
    halo_cross = lax.ppermute(cross_plane, "slab", across)
    packed = (nz, ny // 2, 8 * chunk)
    shapes = [a.shape for a in fields]
    for step_index in range(STEPS):
        first, last = step_index == 0, step_index == STEPS - 1
        arrived = lax.all_to_all(send, "slab", 0, 0, tiled=True)
        kept = () if first else (potential,)
        potential, loads = call(
            functools.partial(solve_kernel, chunk, ny, nz, first),
            [(3 * narrow, ny * nz) if first else (3 * chunk * ny, nz), packed],
            [(2 if first else 1, ny * nz, LANES), (nz * ny // 2, LANES)]
            + ([] if first else [(3 * chunk * ny, LANES)]),
            "sweeps",
            None,
            1 << 22,
            arrived,
            block,
            block_mate,
            block_cross,
            *kept,
        )
        loads = lax.all_to_all(loads, "slab", 0, 0, tiled=True)
        scratch = [(6, 2, rows + 16, wide), sums]
        if last:
            fields = call(
                functools.partial(flow_kernel, True),
                shapes,
                scratch,
                "flow_last",
                None,
                1 << 22,
                *fields,
                halo_mate,
                halo_cross,
                loads,
            )
        else:
            *fields, send, mate_plane, cross_plane = call(
                functools.partial(flow_kernel, False),
                shapes + [(count, ny, LANES), plane, plane],
                scratch + [sums],
                "flow_first",
                7,
                1 << 22,
                *fields,
                halo_mate,
                halo_cross,
                loads,
                zone_labels,
                zone_resistivity_inverse,
            )
            halo_mate = lax.ppermute(mate_plane, "slab", mates)
            halo_cross = lax.ppermute(cross_plane, "slab", across)
    return (*fields, potential.reshape(imposed_induction.shape))


def on_device(*arrays):
    count = lax.axis_size("slab")
    _, chunk, ny, nz = arrays[5].shape
    planes, rows, wide = arrays[1].shape
    narrow = chunk + 2 * (HALO - SWEEPS)
    fits = (
        STEPS == 2
        and planes == 2
        and nz == count
        and count % 2 == 0
        and chunk >= HALO
        and chunk % 8 == 0
        and ny % 16 == 0
        and 4 * narrow == LANES
        and 8 * chunk == LANES
        and nz * ny == 2 * LANES
        and wide % (2 * LANES) == 0
    )
    return window_plan(*arrays) if fits else per_sweep_plan(*arrays)


def solution(mesh):
    return jax.shard_map(
        on_device,
        mesh=mesh,
        in_specs=(
            P(None, ("groups", "slab"), None, None),
            P(("groups", "slab"), None, None),
            P(None, ("groups", "slab"), None, None),
            P(("groups", "slab"), None, None),
            P(),
            P(None, ("groups", "slab"), None, None),
            P(None, ("groups", "slab"), None, None),
            P(None, ("groups", "slab"), None, None),
        ),
        out_specs=(
            P(None, ("groups", "slab"), None, None),
            P(("groups", "slab"), None, None),
            P(None, ("groups", "slab"), None, None),
            P(None, ("groups", "slab"), None, None),
        ),
        check_vma=False,
    )
```

```python
import functools

import jax
import jax.numpy as jnp
from jax import lax
from jax.experimental import pallas as pl
from jax.experimental.pallas import tpu as pltpu
from jax.sharding import PartitionSpec as P

STEPS = 2
SWEEPS = 8


time_step = 0.02
molecular = 0.01
heat_diffuse = 0.01
eddy_coeff = 0.09
prod_coeff = 1.44
dissip_coeff = 1.92
turb_floor = 0.05
coupling = 1.0
thermal_gradient_factor = 0.3


def extended(block, sides, width):
    for axis, dim in sides:
        count = lax.axis_size(axis)
        forward = [(i, i + 1) for i in range(count - 1)]
        backward = [(target, source) for source, target in forward]
        low = lax.ppermute(
            lax.slice_in_dim(block, block.shape[dim] - width, None, axis=dim), axis, forward
        )
        high = lax.ppermute(lax.slice_in_dim(block, 0, width, axis=dim), axis, backward)
        block = jnp.concatenate([low, block, high], axis=dim)
    return block


def reduce_onto_parent(block):
    comps, depth, rows, cols = block.shape
    shaped = block.reshape(comps, depth // 2, 2, rows // 2, 2, cols // 2, 2)
    return jnp.mean(shaped, axis=(2, 4, 6))


def prolong(block):
    comps, depth, rows, cols = block.shape
    wide = jnp.broadcast_to(
        block[:, :, None, :, None, :, None], (comps, depth, 2, rows, 2, cols, 2)
    )
    return wide.reshape(comps, depth * 2, rows * 2, cols * 2)


def cross(left_vec, right_vec):
    return jnp.stack(
        [
            left_vec[1] * right_vec[2] - left_vec[2] * right_vec[1],
            left_vec[2] * right_vec[0] - left_vec[0] * right_vec[2],
            left_vec[0] * right_vec[1] - left_vec[1] * right_vec[0],
        ],
        0,
    )


def neighbours(padded):
    return (
        padded[:, 2:, 1:-1, 1:-1]
        + padded[:, :-2, 1:-1, 1:-1]
        + padded[:, 1:-1, 2:, 1:-1]
        + padded[:, 1:-1, :-2, 1:-1]
        + padded[:, 1:-1, 1:-1, 2:]
        + padded[:, 1:-1, 1:-1, :-2]
    )


def ohmic_admittance(zone_labels, zone_resistivity_inverse, heat_state):
    labels = jnp.arange(zone_resistivity_inverse.shape[0], dtype=jnp.int32)
    onehot = zone_labels[None] == labels[:, None, None, None]
    searched_higher = jnp.sum(
        jnp.where(onehot, zone_resistivity_inverse[:, None, None, None], jnp.float32(0.0)), axis=0
    )
    return (
        searched_higher
        * reduce_onto_parent(jnp.exp(-thermal_gradient_factor * heat_state)[None])[0]
    )


def faces(potential):
    padded = extended(potential, (("slab", 1),), 1)
    return jnp.pad(padded, ((0, 0), (0, 0), (1, 1), (1, 1)))


def relax(coupled, imposed_induction, winding_current, potential):
    conduct = coupled[3]
    motional = cross(coupled[:3], imposed_induction)
    source = conduct * motional + winding_current
    diagonal = 6.0 + coupling * conduct
    for sweep_index in range(SWEEPS):
        potential = (source + neighbours(faces(potential))) / diagonal
    drive_field = motional - coupling * potential
    current = conduct * drive_field + winding_current
    lorentz = cross(current, imposed_induction)
    joule = conduct * jnp.sum(drive_field * drive_field, axis=0)
    return (potential, jnp.concatenate([lorentz, joule[None]], 0))


def advance(padded, lorentz, joule):
    bordered = jnp.pad(padded, ((0, 0), (0, 0), (0, 0), (1, 1)))
    center = bordered[:, 1:-1, 1:-1, 1:-1]
    z_plus = bordered[:, 2:, 1:-1, 1:-1]
    z_minus = bordered[:, :-2, 1:-1, 1:-1]
    y_plus = bordered[:, 1:-1, 2:, 1:-1]
    y_minus = bordered[:, 1:-1, :-2, 1:-1]
    x_plus = bordered[:, 1:-1, 1:-1, 2:]
    x_minus = bordered[:, 1:-1, 1:-1, :-2]
    grad_z = 0.5 * (z_plus - z_minus)
    grad_y = 0.5 * (y_plus - y_minus)
    grad_x = 0.5 * (x_plus - x_minus)
    laplace = z_plus + z_minus + y_plus + y_minus + x_plus + x_minus - 6.0 * center
    kinetic = center[4]
    dissip = center[5]
    transport = center[0] * grad_x + center[1] * grad_y + center[2] * grad_z
    eddy_visc = eddy_coeff * kinetic * kinetic / jnp.maximum(dissip, turb_floor)
    strain = jnp.sum(
        grad_x[:3] * grad_x[:3] + grad_y[:3] * grad_y[:3] + grad_z[:3] * grad_z[:3], axis=0
    )
    produce = eddy_visc * strain
    diffuse = jnp.stack(
        [
            molecular + eddy_visc,
            molecular + eddy_visc,
            molecular + eddy_visc,
            heat_diffuse + eddy_visc / 0.9,
            molecular + eddy_visc,
            molecular + eddy_visc / 1.3,
        ],
        0,
    )
    dissip_source = (
        (prod_coeff * produce - dissip_coeff * dissip) * dissip / jnp.maximum(kinetic, turb_floor)
    )
    source = jnp.concatenate(
        [lorentz, joule[None], (produce - dissip)[None], dissip_source[None]], 0
    )
    return center + time_step * (diffuse * laplace - transport + source)


def flow_step(induction_tables, em_loads):
    padded = extended(induction_tables, (("slab", 1),), 1)
    padded = jnp.pad(padded, ((0, 0), (0, 0), (1, 1), (0, 0)))
    return advance(padded, em_loads[:3], em_loads[3])


def local_coupled(induction_tables, zone_labels, zone_resistivity_inverse):
    conduct = ohmic_admittance(zone_labels, zone_resistivity_inverse, induction_tables[3])
    return jnp.concatenate([reduce_onto_parent(induction_tables[:3]), conduct[None]], 0)


def per_sweep_plan(
    melt_speeds,
    heat_state,
    eddy_quantities,
    zone_labels,
    zone_resistivity_inverse,
    imposed_induction,
    winding_current,
    window_entry_induction_guess,
):
    induction_tables = jnp.concatenate([melt_speeds, heat_state[None], eddy_quantities], 0)
    arrived = (
        lax.all_to_all(
            window_entry_induction_guess, "slab", split_axis=3, concat_axis=1, tiled=True
        ),
        lax.all_to_all(imposed_induction, "slab", split_axis=3, concat_axis=1, tiled=True),
        lax.all_to_all(winding_current, "slab", split_axis=3, concat_axis=1, tiled=True),
    )
    potential = jnp.transpose(arrived[0], (0, 3, 2, 1))
    field_local = jnp.transpose(arrived[1], (0, 3, 2, 1))
    coil_local = jnp.transpose(arrived[2], (0, 3, 2, 1))
    for step_index in range(STEPS):
        coupled = local_coupled(induction_tables, zone_labels, zone_resistivity_inverse)
        potential, em_loads = relax(coupled, field_local, coil_local, potential)
        induction_tables = flow_step(induction_tables, prolong(em_loads))
    potential = lax.all_to_all(
        jnp.transpose(potential, (0, 3, 2, 1)), "slab", split_axis=1, concat_axis=3, tiled=True
    )
    return (induction_tables[:3], induction_tables[3], induction_tables[4:], potential)


HALO = 2 * SWEEPS
LANES = 128


def exact_dot(values, chooser):
    high = values.astype(jnp.bfloat16)
    rest = values - high.astype(jnp.float32)
    middle = rest.astype(jnp.bfloat16)
    low = (rest - middle.astype(jnp.float32)).astype(jnp.bfloat16)
    rows = values.shape[0]
    parts = jnp.dot(
        jnp.concatenate([high, middle, low], 0), chooser, preferred_element_type=jnp.float32
    )
    return parts[:rows] + (parts[rows : 2 * rows] + parts[2 * rows :])


def pair_chooser(wide, weight, transposed):
    shape = (wide // 2, wide) if transposed else (wide, wide // 2)
    fine = lax.broadcasted_iota(jnp.int32, shape, 1 if transposed else 0)
    coarse = lax.broadcasted_iota(jnp.int32, shape, 0 if transposed else 1)
    picked = lax.shift_right_logical(fine, 1) == coarse
    return jnp.where(picked, jnp.float32(weight), jnp.float32(0.0)).astype(jnp.bfloat16)


def pack_windows(sums_ref, labels_ref, table_ref, send_ref, halo):
    tiles, rows, _ = sums_ref.shape
    wide = tiles * LANES
    count, ny = send_ref.shape[0], labels_ref.shape[1]
    paired = jnp.concatenate(
        [
            sums_ref[t, pl.ds(0, rows // 2, stride=2), :] + sums_ref[t, pl.ds(1, rows // 2, stride=2), :]
            for t in range(tiles)
        ],
        1,
    )
    coarse = exact_dot(paired, pair_chooser(wide, 0.125, False))
    labels = labels_ref[0]
    admittance = jnp.zeros(labels.shape, jnp.float32)
    for region in range(table_ref.shape[0]):
        admittance = jnp.where(labels == region, table_ref[region], admittance)
    coupled = jnp.concatenate([coarse[: 3 * ny], coarse[3 * ny :] * admittance], 0)
    nx = wide // 2
    chunk = nx // count
    window = chunk + 2 * halo
    padded = jnp.concatenate([coupled, jnp.zeros((4 * ny, LANES), jnp.float32)], 1)
    padded = pltpu.roll(padded, halo, 1)
    for target in range(count):
        start = target * chunk
        joined = jnp.concatenate(
            [padded[f * ny : (f + 1) * ny, start : start + window] for f in range(4)], 1
        )
        send_ref[target, :ny, :] = joined[:, :LANES]
        if 4 * window > LANES:
            half = ny // 2
            send_ref[target, ny:, :] = jnp.concatenate(
                [joined[:half, LANES:], joined[half:, LANES:]], 1
            )


def edge_kernel(vel_ref, heat_ref, turb_ref, guess_ref, applied_ref, coil_ref, mate_ref, cross_ref, flat_ref, sems):
    odd = lax.rem(lax.axis_index("slab"), 2)
    rows = heat_ref.shape[1]
    moves = []
    for f in range(6):
        for which, (out_ref, plane) in enumerate(((mate_ref, 1 - odd), (cross_ref, odd))):
            if f < 3:
                start = vel_ref.at[f, plane]
            elif f == 3:
                start = heat_ref.at[plane]
            else:
                start = turb_ref.at[f - 4, plane]
            move = pltpu.make_async_copy(
                start, out_ref.at[pl.ds(f * rows, rows)], sems.at[2 * f + which]
            )
            move.start()
            moves.append(move)
    pairs, nz = guess_ref.shape
    chunk = (mate_ref.shape[0] - 6 * rows) // 5
    ny = pairs // (3 * chunk)
    lanes = ny * nz
    for kind, ref in enumerate((guess_ref, applied_ref, coil_ref)):
        flat_ref[:, kind * nz : (kind + 1) * nz] = ref[...]
    lines = [flat_ref[pl.ds(y, 3 * chunk, stride=ny), :] for y in range(ny)]
    for kind in range(3):
        packed = jnp.concatenate([line[:, kind * nz : (kind + 1) * nz] for line in lines], 1)
        for c in range(3):
            row, lane = block_spot(3 * kind + c, rows, chunk, lanes)
            piece = packed[c * chunk : (c + 1) * chunk]
            mate_ref[row, lane] = piece
            cross_ref[row, lane] = piece
    for move in moves:
        move.wait()


def block_spot(index, rows, chunk, lanes):
    row = 6 * rows + (index % 5) * chunk
    return slice(row, row + chunk), slice(index // 5 * lanes, (index // 5 + 1) * lanes)


def open_kernel(vel_ref, heat_ref, labels_ref, table_ref, send_ref, sums_ref):
    rows = heat_ref.shape[1]
    for t in range(sums_ref.shape[0]):
        at = slice(t * LANES, (t + 1) * LANES)
        for c in range(3):
            sums_ref[t, c * rows : (c + 1) * rows, :] = vel_ref[c, 0, :, at] + vel_ref[c, 1, :, at]
        sums_ref[t, 3 * rows :, :] = jnp.exp(
            -thermal_gradient_factor * heat_ref[0, :, at]
        ) + jnp.exp(-thermal_gradient_factor * heat_ref[1, :, at])
    pack_windows(sums_ref, labels_ref, table_ref, send_ref, HALO)


def solve_kernel(chunk, ny, nz, rows, first, *refs):
    if first:
        recv_ref, block_ref, mate_ref, cross_ref, pot_out, send_ref, wide_ref, turn_ref = refs
        halo = HALO
    else:
        recv_ref, block_ref, mate_ref, cross_ref, pot_in, pot_out, send_ref = refs[:7]
        wide_ref, turn_ref, flat_ref = refs[7:]
        halo = HALO - SWEEPS
    window = chunk + 2 * halo
    place = lax.axis_index("slab")
    count = lax.axis_size("slab")
    odd = lax.rem(place, 2)
    half = ny // 2
    for z in range(nz):
        wide_ref[0, pl.ds(z, ny, stride=nz), :] = recv_ref[z, :ny, :]
        if 4 * window > LANES:
            tail = recv_ref[z, ny:, :]
            wide_ref[1, pl.ds(z, half, stride=nz), :] = tail
            wide_ref[1, pl.ds(half * nz + z, half, stride=nz), :] = pltpu.roll(tail, LANES // 2, 1)
    turned = jnp.concatenate([jnp.transpose(wide_ref[t]) for t in range(wide_ref.shape[0])], 0)
    velocity = [turned[c * window : (c + 1) * window] for c in range(3)]
    conduct = turned[3 * window : 4 * window]

    def windowed(kind):
        found = []
        for c in range(3):
            row, lane = block_spot(3 * kind + c, rows, chunk, ny * nz)
            mate, cross_side = mate_ref[row, lane], cross_ref[row, lane]
            low = jnp.where(odd == 0, cross_side, mate)
            high = jnp.where(odd == 0, mate, cross_side)
            found.append(
                jnp.concatenate(
                    [low[chunk - halo :], block_ref[row, lane], high[:halo]], 0
                )
            )
        return found

    applied, coil = windowed(1), windowed(2)
    potential = jnp.concatenate(windowed(0), 0) if first else pot_in[...]
    motional = [
        velocity[1] * applied[2] - velocity[2] * applied[1],
        velocity[2] * applied[0] - velocity[0] * applied[2],
        velocity[0] * applied[1] - velocity[1] * applied[0],
    ]
    where_x = place * chunk - halo + lax.broadcasted_iota(jnp.int32, (window, ny * nz), 0)
    inside = (where_x >= 0) & (where_x < count * chunk)
    inverse = jnp.where(inside, 1.0 / (6.0 + coupling * conduct), 0.0)
    source = jnp.concatenate([conduct * motional[c] + coil[c] for c in range(3)], 0)
    inverse = jnp.concatenate([inverse] * 3, 0)
    source = source * inverse
    shape = potential.shape
    lane = lax.broadcasted_iota(jnp.int32, shape, 1)
    column = lax.rem(lane, nz)
    for sweep in range(SWEEPS):
        around = pltpu.roll(potential, 1, 0) + pltpu.roll(potential, shape[0] - 1, 0)
        around += jnp.where(column == 0, 0.0, pltpu.roll(potential, 1, 1))
        around += jnp.where(column == nz - 1, 0.0, pltpu.roll(potential, shape[1] - 1, 1))
        around += jnp.where(lane < nz, 0.0, pltpu.roll(potential, nz, 1))
        around += jnp.where(lane >= shape[1] - nz, 0.0, pltpu.roll(potential, shape[1] - nz, 1))
        potential = source + around * inverse
    own = [potential[c * window + halo : c * window + halo + chunk] for c in range(3)]
    if first:
        keep = chunk + 2 * (halo - SWEEPS)
        for c in range(3):
            pot_out[c * keep : (c + 1) * keep, :] = potential[
                c * window + SWEEPS : c * window + SWEEPS + keep
            ]
    else:
        together = jnp.concatenate(own, 0)
        lanes = ny * nz
        for y in range(ny):
            line = pltpu.roll(together, lanes - y * nz, 1) if y else together
            flat_ref[pl.ds(y, 3 * chunk, stride=ny), :] = line[:, :LANES]
        pot_out[...] = flat_ref[:, :nz]
    mine = slice(halo, halo + chunk)
    conduct_own = conduct[mine]
    applied_own = [a[mine] for a in applied]
    drive = [motional[c][mine] - coupling * own[c] for c in range(3)]
    current = [conduct_own * drive[c] + coil[c][mine] for c in range(3)]
    loads = [
        current[1] * applied_own[2] - current[2] * applied_own[1],
        current[2] * applied_own[0] - current[0] * applied_own[2],
        current[0] * applied_own[1] - current[1] * applied_own[0],
        conduct_own * (drive[0] * drive[0] + drive[1] * drive[1] + drive[2] * drive[2]),
    ]
    loads = jnp.concatenate(loads, 0)
    middle = half * nz
    turn_ref[...] = jnp.transpose(jnp.concatenate([loads[:, :middle], loads[:, middle:]], 0))
    for z in range(nz):
        send_ref[z] = turn_ref[pl.ds(z, half, stride=nz), :]


def flow_kernel(last, *refs):
    vel_ref, heat_ref, turb_ref, mate_ref, cross_ref, recv_ref = refs[:6]
    if last:
        vel_out, heat_out, turb_out, bordered_ref, loads_ref = refs[6:]
    else:
        labels_ref, table_ref = refs[6:8]
        vel_out, heat_out, turb_out, send_ref, mate_out, cross_out = refs[8:14]
        bordered_ref, loads_ref, sums_ref = refs[14:]
    odd = lax.rem(lax.axis_index("slab"), 2)
    rows, wide = heat_ref.shape[1:]
    count, half, packed = recv_ref.shape
    chunk = packed // 8
    edge = jnp.zeros((8, wide), jnp.float32)
    for f in range(6):
        for plane in range(2):
            bordered_ref[f, plane, 0:8, :] = edge
            bordered_ref[f, plane, 8 + rows :, :] = edge
            if f < 3:
                block = vel_ref[f, plane]
            elif f == 3:
                block = heat_ref[plane]
            else:
                block = turb_ref[f - 4, plane]
            bordered_ref[f, plane, 8 : 8 + rows, :] = block
    stacked = []
    for f in range(4):
        for side in range(2):
            at = (side * 4 + f) * chunk
            stacked.append(
                jnp.concatenate([recv_ref[s, :, at : at + chunk] for s in range(count)], 1)
            )
    spread = exact_dot(jnp.concatenate(stacked, 0), pair_chooser(wide, 1.0, True))
    for t in range(wide // LANES):
        part = spread[:, t * LANES : (t + 1) * LANES]
        loads_ref[t, pl.ds(0, 2 * rows, stride=2), :] = part
        loads_ref[t, pl.ds(1, 2 * rows, stride=2), :] = part
    lane = lax.broadcasted_iota(jnp.int32, (8, wide), 1)
    first_lane, last_lane = lane == 0, lane == wide - 1
    for top in range(0, rows, 8):
        tile = slice(top, top + 8)
        for plane in range(2):
            center = [bordered_ref[f, plane, 8 + top : 16 + top, :] for f in range(6)]
            kinetic, dissip = center[4], center[5]
            eddy_visc = eddy_coeff * kinetic * kinetic / jnp.maximum(dissip, turb_floor)
            strain = jnp.zeros((8, wide), jnp.float32)
            for f in range(6):
                here = center[f]
                spot = slice(f * rows + top, f * rows + top + 8)
                mate, cross_side = mate_ref[spot, :], cross_ref[spot, :]
                other = bordered_ref[f, 1 - plane, 8 + top : 16 + top, :]
                if plane == 0:
                    z_minus, z_plus = jnp.where(odd == 0, cross_side, mate), other
                else:
                    z_minus, z_plus = other, jnp.where(odd == 0, mate, cross_side)
                y_minus = bordered_ref[f, plane, 7 + top : 15 + top, :]
                y_plus = bordered_ref[f, plane, 9 + top : 17 + top, :]
                x_minus = jnp.where(first_lane, 0.0, pltpu.roll(here, 1, 1))
                x_plus = jnp.where(last_lane, 0.0, pltpu.roll(here, wide - 1, 1))
                grad_z = 0.5 * (z_plus - z_minus)
                grad_y = 0.5 * (y_plus - y_minus)
                grad_x = 0.5 * (x_plus - x_minus)
                laplace = z_plus + z_minus + y_plus + y_minus + x_plus + x_minus - 6.0 * here
                transport = center[0] * grad_x + center[1] * grad_y + center[2] * grad_z
                if f < 3:
                    strain += grad_x * grad_x + grad_y * grad_y + grad_z * grad_z
                    diffuse = molecular + eddy_visc
                    source = jnp.concatenate(
                        [
                            loads_ref[t, f * rows + top : f * rows + top + 8, :]
                            for t in range(wide // LANES)
                        ],
                        1,
                    )
                elif f == 3:
                    diffuse = heat_diffuse + eddy_visc * (1.0 / 0.9)
                    source = jnp.concatenate(
                        [
                            loads_ref[t, f * rows + top : f * rows + top + 8, :]
                            for t in range(wide // LANES)
                        ],
                        1,
                    )
                elif f == 4:
                    produce = eddy_visc * strain
                    diffuse = molecular + eddy_visc
                    source = produce - dissip
                else:
                    diffuse = molecular + eddy_visc * (1.0 / 1.3)
                    source = (
                        (prod_coeff * produce - dissip_coeff * dissip)
                        * dissip
                        / jnp.maximum(kinetic, turb_floor)
                    )
                fresh = here + time_step * (diffuse * laplace - transport + source)
                if f < 3:
                    vel_out[f, plane, tile, :] = fresh
                elif f == 3:
                    heat_out[plane, tile, :] = fresh
                else:
                    turb_out[f - 4, plane, tile, :] = fresh
                if not last and f < 4:
                    part = jnp.exp(-thermal_gradient_factor * fresh) if f == 3 else fresh
                    spot = slice(f * rows + top, f * rows + top + 8)
                    for t in range(wide // LANES):
                        piece = part[:, t * LANES : (t + 1) * LANES]
                        sums_ref[t, spot, :] = piece if plane == 0 else sums_ref[t, spot, :] + piece
    if last:
        return
    outs = [(vel_out, 0), (vel_out, 1), (vel_out, 2), (heat_out, None), (turb_out, 0), (turb_out, 1)]
    for f, (ref, comp) in enumerate(outs):
        if comp is None:
            mate_out[f * rows : (f + 1) * rows, :] = ref[1 - odd]
            cross_out[f * rows : (f + 1) * rows, :] = ref[odd]
        else:
            mate_out[f * rows : (f + 1) * rows, :] = ref[comp, 1 - odd]
            cross_out[f * rows : (f + 1) * rows, :] = ref[comp, odd]
    pack_windows(sums_ref, labels_ref, table_ref, send_ref, HALO - SWEEPS)


def call(kernel, outs, scratch, name, spaces, grant, cost, *operands):
    vmem = pl.BlockSpec(memory_space=pltpu.VMEM)
    special = {"s": pl.BlockSpec(memory_space=pltpu.SMEM), "a": pl.BlockSpec(memory_space=pl.ANY)}
    return pl.pallas_call(
        kernel,
        out_shape=[jax.ShapeDtypeStruct(s, jnp.float32) for s in outs],
        in_specs=[special.get(spaces.get(i), vmem) for i in range(len(operands))],
        out_specs=[vmem] * len(outs),
        scratch_shapes=[pltpu.VMEM(s, jnp.float32) if isinstance(s, tuple) else s for s in scratch],
        name=name,
        cost_estimate=pl.CostEstimate(flops=cost, bytes_accessed=cost, transcendentals=0),
        compiler_params=pltpu.CompilerParams(vmem_limit_bytes=grant << 20),
    )(*operands)


def beside(block):
    count = lax.axis_size("slab")
    mates = [(i, i ^ 1) for i in range(count)]
    across = [(i, i + 1) for i in range(1, count - 1, 2)]
    across = across + [(b, a) for a, b in across]
    return mates, across


def window_plan(
    melt_speeds,
    heat_state,
    eddy_quantities,
    zone_labels,
    zone_resistivity_inverse,
    imposed_induction,
    winding_current,
    window_entry_induction_guess,
):
    count = lax.axis_size("slab")
    _, chunk, ny, nz = imposed_induction.shape
    _, rows, wide = heat_state.shape
    mates, across = beside(None)
    flat = [
        a.reshape(3 * chunk * ny, nz)
        for a in (window_entry_induction_guess, imposed_induction, winding_current)
    ]
    window, narrow = chunk + 2 * HALO, chunk + 2 * (HALO - SWEEPS)
    tall = ny + ny // 2 if 4 * window > LANES else ny
    edge = (6 * rows, wide)
    joint = (6 * rows + 5 * chunk, wide)
    sums = (wide // LANES, 4 * rows, LANES)
    fields = (melt_speeds, heat_state, eddy_quantities)
    mate, cross_side = call(
        edge_kernel,
        [joint, joint],
        [(3 * chunk * ny, LANES), pltpu.SemaphoreType.DMA((12,))],
        "edges",
        {0: "a", 1: "a", 2: "a"},
        8,
        1 << 20,
        *fields,
        *flat,
    )
    block = mate
    mate = lax.ppermute(mate, "slab", mates)
    cross_side = lax.ppermute(cross_side, "slab", across)
    block_mate, block_cross = mate, cross_side
    (send,) = call(
        open_kernel,
        [(count, tall, LANES)],
        [sums],
        "open_windows",
        {3: "s"},
        8,
        1 << 22,
        melt_speeds,
        heat_state,
        zone_labels,
        zone_resistivity_inverse,
    )
    packed = (nz, ny // 2, 8 * chunk)
    shapes = [a.shape for a in fields]
    for step_index in range(STEPS):
        first, last = step_index == 0, step_index == STEPS - 1
        arrived = lax.all_to_all(send, "slab", 0, 0, tiled=True)
        kept = () if first else (potential,)
        potential, loads = call(
            functools.partial(solve_kernel, chunk, ny, nz, rows, first),
            [(3 * narrow, ny * nz) if first else (3 * chunk * ny, nz), packed],
            [(2 if first else 1, ny * nz, LANES), (nz * ny // 2, LANES)]
            + ([] if first else [(3 * chunk * ny, LANES)]),
            "sweeps",
            {},
            8,
            1 << 22,
            arrived,
            block,
            block_mate,
            block_cross,
            *kept,
        )
        loads = lax.all_to_all(loads, "slab", 0, 0, tiled=True)
        scratch = [(6, 2, rows + 16, wide), sums]
        if last:
            fields = call(
                functools.partial(flow_kernel, True),
                shapes,
                scratch,
                "flow_last",
                {},
                12,
                1 << 22,
                *fields,
                mate,
                cross_side,
                loads,
            )
        else:
            *fields, send, mate, cross_side = call(
                functools.partial(flow_kernel, False),
                shapes + [(count, ny, LANES), edge, edge],
                scratch + [sums],
                "flow_first",
                {7: "s"},
                12,
                1 << 22,
                *fields,
                mate,
                cross_side,
                loads,
                zone_labels,
                zone_resistivity_inverse,
            )
            mate = lax.ppermute(mate, "slab", mates)
            cross_side = lax.ppermute(cross_side, "slab", across)
    return (*fields, potential.reshape(imposed_induction.shape))


def on_device(*arrays):
    count = lax.axis_size("slab")
    _, chunk, ny, nz = arrays[5].shape
    planes, rows, wide = arrays[1].shape
    narrow = chunk + 2 * (HALO - SWEEPS)
    fits = (
        STEPS == 2
        and planes == 2
        and nz == count
        and count % 2 == 0
        and chunk >= HALO
        and chunk % 8 == 0
        and ny % 16 == 0
        and 4 * narrow == LANES
        and 8 * chunk == LANES
        and nz * ny == 2 * LANES
        and wide == 2 * ny * nz
    )
    return window_plan(*arrays) if fits else per_sweep_plan(*arrays)


def solution(mesh):
    return jax.shard_map(
        on_device,
        mesh=mesh,
        in_specs=(
            P(None, ("groups", "slab"), None, None),
            P(("groups", "slab"), None, None),
            P(None, ("groups", "slab"), None, None),
            P(("groups", "slab"), None, None),
            P(),
            P(None, ("groups", "slab"), None, None),
            P(None, ("groups", "slab"), None, None),
            P(None, ("groups", "slab"), None, None),
        ),
        out_specs=(
            P(None, ("groups", "slab"), None, None),
            P(("groups", "slab"), None, None),
            P(None, ("groups", "slab"), None, None),
            P(None, ("groups", "slab"), None, None),
        ),
        check_vma=False,
    )
```

```python
import functools

import jax
import jax.numpy as jnp
from jax import lax
from jax.experimental import pallas as pl
from jax.experimental.pallas import tpu as pltpu
from jax.sharding import PartitionSpec as P

STEPS = 2
SWEEPS = 8


time_step = 0.02
molecular = 0.01
heat_diffuse = 0.01
eddy_coeff = 0.09
prod_coeff = 1.44
dissip_coeff = 1.92
turb_floor = 0.05
coupling = 1.0
thermal_gradient_factor = 0.3


def extended(block, sides, width):
    for axis, dim in sides:
        count = lax.axis_size(axis)
        forward = [(i, i + 1) for i in range(count - 1)]
        backward = [(target, source) for source, target in forward]
        low = lax.ppermute(
            lax.slice_in_dim(block, block.shape[dim] - width, None, axis=dim), axis, forward
        )
        high = lax.ppermute(lax.slice_in_dim(block, 0, width, axis=dim), axis, backward)
        block = jnp.concatenate([low, block, high], axis=dim)
    return block


def reduce_onto_parent(block):
    comps, depth, rows, cols = block.shape
    shaped = block.reshape(comps, depth // 2, 2, rows // 2, 2, cols // 2, 2)
    return jnp.mean(shaped, axis=(2, 4, 6))


def prolong(block):
    comps, depth, rows, cols = block.shape
    wide = jnp.broadcast_to(
        block[:, :, None, :, None, :, None], (comps, depth, 2, rows, 2, cols, 2)
    )
    return wide.reshape(comps, depth * 2, rows * 2, cols * 2)


def cross(left_vec, right_vec):
    return jnp.stack(
        [
            left_vec[1] * right_vec[2] - left_vec[2] * right_vec[1],
            left_vec[2] * right_vec[0] - left_vec[0] * right_vec[2],
            left_vec[0] * right_vec[1] - left_vec[1] * right_vec[0],
        ],
        0,
    )


def neighbours(padded):
    return (
        padded[:, 2:, 1:-1, 1:-1]
        + padded[:, :-2, 1:-1, 1:-1]
        + padded[:, 1:-1, 2:, 1:-1]
        + padded[:, 1:-1, :-2, 1:-1]
        + padded[:, 1:-1, 1:-1, 2:]
        + padded[:, 1:-1, 1:-1, :-2]
    )


def ohmic_admittance(zone_labels, zone_resistivity_inverse, heat_state):
    labels = jnp.arange(zone_resistivity_inverse.shape[0], dtype=jnp.int32)
    onehot = zone_labels[None] == labels[:, None, None, None]
    searched_higher = jnp.sum(
        jnp.where(onehot, zone_resistivity_inverse[:, None, None, None], jnp.float32(0.0)), axis=0
    )
    return (
        searched_higher
        * reduce_onto_parent(jnp.exp(-thermal_gradient_factor * heat_state)[None])[0]
    )


def faces(potential):
    padded = extended(potential, (("slab", 1),), 1)
    return jnp.pad(padded, ((0, 0), (0, 0), (1, 1), (1, 1)))


def relax(coupled, imposed_induction, winding_current, potential):
    conduct = coupled[3]
    motional = cross(coupled[:3], imposed_induction)
    source = conduct * motional + winding_current
    diagonal = 6.0 + coupling * conduct
    for sweep_index in range(SWEEPS):
        potential = (source + neighbours(faces(potential))) / diagonal
    drive_field = motional - coupling * potential
    current = conduct * drive_field + winding_current
    lorentz = cross(current, imposed_induction)
    joule = conduct * jnp.sum(drive_field * drive_field, axis=0)
    return (potential, jnp.concatenate([lorentz, joule[None]], 0))


def advance(padded, lorentz, joule):
    bordered = jnp.pad(padded, ((0, 0), (0, 0), (0, 0), (1, 1)))
    center = bordered[:, 1:-1, 1:-1, 1:-1]
    z_plus = bordered[:, 2:, 1:-1, 1:-1]
    z_minus = bordered[:, :-2, 1:-1, 1:-1]
    y_plus = bordered[:, 1:-1, 2:, 1:-1]
    y_minus = bordered[:, 1:-1, :-2, 1:-1]
    x_plus = bordered[:, 1:-1, 1:-1, 2:]
    x_minus = bordered[:, 1:-1, 1:-1, :-2]
    grad_z = 0.5 * (z_plus - z_minus)
    grad_y = 0.5 * (y_plus - y_minus)
    grad_x = 0.5 * (x_plus - x_minus)
    laplace = z_plus + z_minus + y_plus + y_minus + x_plus + x_minus - 6.0 * center
    kinetic = center[4]
    dissip = center[5]
    transport = center[0] * grad_x + center[1] * grad_y + center[2] * grad_z
    eddy_visc = eddy_coeff * kinetic * kinetic / jnp.maximum(dissip, turb_floor)
    strain = jnp.sum(
        grad_x[:3] * grad_x[:3] + grad_y[:3] * grad_y[:3] + grad_z[:3] * grad_z[:3], axis=0
    )
    produce = eddy_visc * strain
    diffuse = jnp.stack(
        [
            molecular + eddy_visc,
            molecular + eddy_visc,
            molecular + eddy_visc,
            heat_diffuse + eddy_visc / 0.9,
            molecular + eddy_visc,
            molecular + eddy_visc / 1.3,
        ],
        0,
    )
    dissip_source = (
        (prod_coeff * produce - dissip_coeff * dissip) * dissip / jnp.maximum(kinetic, turb_floor)
    )
    source = jnp.concatenate(
        [lorentz, joule[None], (produce - dissip)[None], dissip_source[None]], 0
    )
    return center + time_step * (diffuse * laplace - transport + source)


def flow_step(induction_tables, em_loads):
    padded = extended(induction_tables, (("slab", 1),), 1)
    padded = jnp.pad(padded, ((0, 0), (0, 0), (1, 1), (0, 0)))
    return advance(padded, em_loads[:3], em_loads[3])


def local_coupled(induction_tables, zone_labels, zone_resistivity_inverse):
    conduct = ohmic_admittance(zone_labels, zone_resistivity_inverse, induction_tables[3])
    return jnp.concatenate([reduce_onto_parent(induction_tables[:3]), conduct[None]], 0)


def per_sweep_plan(
    melt_speeds,
    heat_state,
    eddy_quantities,
    zone_labels,
    zone_resistivity_inverse,
    imposed_induction,
    winding_current,
    window_entry_induction_guess,
):
    induction_tables = jnp.concatenate([melt_speeds, heat_state[None], eddy_quantities], 0)
    arrived = (
        lax.all_to_all(
            window_entry_induction_guess, "slab", split_axis=3, concat_axis=1, tiled=True
        ),
        lax.all_to_all(imposed_induction, "slab", split_axis=3, concat_axis=1, tiled=True),
        lax.all_to_all(winding_current, "slab", split_axis=3, concat_axis=1, tiled=True),
    )
    potential = jnp.transpose(arrived[0], (0, 3, 2, 1))
    field_local = jnp.transpose(arrived[1], (0, 3, 2, 1))
    coil_local = jnp.transpose(arrived[2], (0, 3, 2, 1))
    for step_index in range(STEPS):
        coupled = local_coupled(induction_tables, zone_labels, zone_resistivity_inverse)
        potential, em_loads = relax(coupled, field_local, coil_local, potential)
        induction_tables = flow_step(induction_tables, prolong(em_loads))
    potential = lax.all_to_all(
        jnp.transpose(potential, (0, 3, 2, 1)), "slab", split_axis=1, concat_axis=3, tiled=True
    )
    return (induction_tables[:3], induction_tables[3], induction_tables[4:], potential)


HALO = 2 * SWEEPS
LANES = 128


def exact_dot(values, chooser):
    high = values.astype(jnp.bfloat16)
    rest = values - high.astype(jnp.float32)
    middle = rest.astype(jnp.bfloat16)
    low = (rest - middle.astype(jnp.float32)).astype(jnp.bfloat16)
    rows = values.shape[0]
    parts = jnp.dot(
        jnp.concatenate([high, middle, low], 0), chooser, preferred_element_type=jnp.float32
    )
    return parts[:rows] + (parts[rows : 2 * rows] + parts[2 * rows :])


def pair_chooser(wide, weight, transposed):
    shape = (wide // 2, wide) if transposed else (wide, wide // 2)
    fine = lax.broadcasted_iota(jnp.int32, shape, 1 if transposed else 0)
    coarse = lax.broadcasted_iota(jnp.int32, shape, 0 if transposed else 1)
    picked = lax.shift_right_logical(fine, 1) == coarse
    return jnp.where(picked, jnp.float32(weight), jnp.float32(0.0)).astype(jnp.bfloat16)


def pack_windows(sums_ref, labels_ref, table_ref, send_ref, halo):
    tiles, rows, _ = sums_ref.shape
    wide = tiles * LANES
    count, ny = send_ref.shape[0], labels_ref.shape[1]
    paired = jnp.concatenate(
        [
            sums_ref[t, pl.ds(0, rows // 2, stride=2), :] + sums_ref[t, pl.ds(1, rows // 2, stride=2), :]
            for t in range(tiles)
        ],
        1,
    )
    coarse = exact_dot(paired, pair_chooser(wide, 0.125, False))
    labels = labels_ref[0]
    admittance = jnp.zeros(labels.shape, jnp.float32)
    for region in range(table_ref.shape[0]):
        admittance = jnp.where(labels == region, table_ref[region], admittance)
    coupled = jnp.concatenate([coarse[: 3 * ny], coarse[3 * ny :] * admittance], 0)
    nx = wide // 2
    chunk = nx // count
    window = chunk + 2 * halo
    padded = jnp.concatenate([coupled, jnp.zeros((4 * ny, LANES), jnp.float32)], 1)
    padded = pltpu.roll(padded, halo, 1)
    for target in range(count):
        start = target * chunk
        joined = jnp.concatenate(
            [padded[f * ny : (f + 1) * ny, start : start + window] for f in range(4)], 1
        )
        send_ref[target, :ny, :] = joined[:, :LANES]
        if 4 * window > LANES:
            half = ny // 2
            send_ref[target, ny:, :] = jnp.concatenate(
                [joined[:half, LANES:], joined[half:, LANES:]], 1
            )


def edge_kernel(
    vel_ref,
    heat_ref,
    turb_ref,
    guess_ref,
    applied_ref,
    coil_ref,
    mate_ref,
    cross_ref,
    vel_out,
    heat_out,
    turb_out,
    flat_ref,
    raw_ref,
    sems,
):
    odd = lax.rem(lax.axis_index("slab"), 2)
    rows = heat_ref.shape[1]
    pairs = [(guess_ref, raw_ref.at[0]), (applied_ref, raw_ref.at[1]), (coil_ref, raw_ref.at[2])]
    pairs += [(vel_ref, vel_out), (heat_ref, heat_out), (turb_ref, turb_out)]
    moves = [pltpu.make_async_copy(a, b, sems.at[i]) for i, (a, b) in enumerate(pairs)]
    for move in moves:
        move.start()
    for move in moves[:3]:
        move.wait()
    total, nz = guess_ref.shape
    chunk = (mate_ref.shape[0] - 6 * rows) // 5
    ny = total // (3 * chunk)
    lanes = ny * nz
    for kind in range(3):
        flat_ref[:, kind * nz : (kind + 1) * nz] = raw_ref[kind]
    lines = [flat_ref[pl.ds(y, 3 * chunk, stride=ny), :] for y in range(ny)]
    for kind in range(3):
        packed = jnp.concatenate([line[:, kind * nz : (kind + 1) * nz] for line in lines], 1)
        for c in range(3):
            row, lane = block_spot(3 * kind + c, rows, chunk, lanes)
            piece = packed[c * chunk : (c + 1) * chunk]
            mate_ref[row, lane] = piece
            cross_ref[row, lane] = piece
    for move in moves[3:]:
        move.wait()
    split_planes(odd, vel_out, heat_out, turb_out, mate_ref, cross_ref)


def split_planes(odd, vel_ref, heat_ref, turb_ref, mate_ref, cross_ref):
    rows = heat_ref.shape[1]
    for f in range(6):
        spot = slice(f * rows, (f + 1) * rows)
        for ref, plane in ((mate_ref, 1 - odd), (cross_ref, odd)):
            if f < 3:
                ref[spot, :] = vel_ref[f, plane]
            elif f == 3:
                ref[spot, :] = heat_ref[plane]
            else:
                ref[spot, :] = turb_ref[f - 4, plane]


def block_spot(index, rows, chunk, lanes):
    row = 6 * rows + (index % 5) * chunk
    return slice(row, row + chunk), slice(index // 5 * lanes, (index // 5 + 1) * lanes)


def open_kernel(vel_ref, heat_ref, labels_ref, table_ref, send_ref, sums_ref):
    rows = heat_ref.shape[1]
    for t in range(sums_ref.shape[0]):
        at = slice(t * LANES, (t + 1) * LANES)
        for c in range(3):
            sums_ref[t, c * rows : (c + 1) * rows, :] = vel_ref[c, 0, :, at] + vel_ref[c, 1, :, at]
        sums_ref[t, 3 * rows :, :] = jnp.exp(
            -thermal_gradient_factor * heat_ref[0, :, at]
        ) + jnp.exp(-thermal_gradient_factor * heat_ref[1, :, at])
    pack_windows(sums_ref, labels_ref, table_ref, send_ref, HALO)


def solve_kernel(chunk, ny, nz, rows, first, *refs):
    if first:
        recv_ref, block_ref, mate_ref, cross_ref, pot_out, send_ref, wide_ref, turn_ref = refs
        halo = HALO
    else:
        recv_ref, block_ref, mate_ref, cross_ref, pot_in, pot_out, send_ref = refs[:7]
        wide_ref, turn_ref = refs[7:]
        halo = HALO - SWEEPS
    window = chunk + 2 * halo
    place = lax.axis_index("slab")
    count = lax.axis_size("slab")
    odd = lax.rem(place, 2)
    half = ny // 2
    for z in range(nz):
        wide_ref[0, pl.ds(z, ny, stride=nz), :] = recv_ref[z, :ny, :]
        if 4 * window > LANES:
            tail = recv_ref[z, ny:, :]
            wide_ref[1, pl.ds(z, half, stride=nz), :] = tail
            wide_ref[1, pl.ds(half * nz + z, half, stride=nz), :] = pltpu.roll(tail, LANES // 2, 1)
    turned = jnp.concatenate([jnp.transpose(wide_ref[t]) for t in range(wide_ref.shape[0])], 0)
    velocity = [turned[c * window : (c + 1) * window] for c in range(3)]
    conduct = turned[3 * window : 4 * window]

    def windowed(kind):
        found = []
        for c in range(3):
            row, lane = block_spot(3 * kind + c, rows, chunk, ny * nz)
            mate, cross_side = mate_ref[row, lane], cross_ref[row, lane]
            low = jnp.where(odd == 0, cross_side, mate)
            high = jnp.where(odd == 0, mate, cross_side)
            found.append(
                jnp.concatenate(
                    [low[chunk - halo :], block_ref[row, lane], high[:halo]], 0
                )
            )
        return found

    applied, coil = windowed(1), windowed(2)
    potential = jnp.concatenate(windowed(0), 0) if first else pot_in[...]
    motional = [
        velocity[1] * applied[2] - velocity[2] * applied[1],
        velocity[2] * applied[0] - velocity[0] * applied[2],
        velocity[0] * applied[1] - velocity[1] * applied[0],
    ]
    where_x = place * chunk - halo + lax.broadcasted_iota(jnp.int32, (window, ny * nz), 0)
    inside = (where_x >= 0) & (where_x < count * chunk)
    inverse = jnp.where(inside, 1.0 / (6.0 + coupling * conduct), 0.0)
    source = jnp.concatenate([conduct * motional[c] + coil[c] for c in range(3)], 0)
    inverse = jnp.concatenate([inverse] * 3, 0)
    source = source * inverse
    shape = potential.shape
    lane = lax.broadcasted_iota(jnp.int32, shape, 1)
    column = lax.rem(lane, nz)
    for sweep in range(SWEEPS):
        around = pltpu.roll(potential, 1, 0) + pltpu.roll(potential, shape[0] - 1, 0)
        around += jnp.where(column == 0, 0.0, pltpu.roll(potential, 1, 1))
        around += jnp.where(column == nz - 1, 0.0, pltpu.roll(potential, shape[1] - 1, 1))
        around += jnp.where(lane < nz, 0.0, pltpu.roll(potential, nz, 1))
        around += jnp.where(lane >= shape[1] - nz, 0.0, pltpu.roll(potential, shape[1] - nz, 1))
        potential = source + around * inverse
    own = [potential[c * window + halo : c * window + halo + chunk] for c in range(3)]
    if first:
        keep = chunk + 2 * (halo - SWEEPS)
        for c in range(3):
            pot_out[c * keep : (c + 1) * keep, :] = potential[
                c * window + SWEEPS : c * window + SWEEPS + keep
            ]
    else:
        pot_out[...] = jnp.concatenate(own, 0)
    mine = slice(halo, halo + chunk)
    conduct_own = conduct[mine]
    applied_own = [a[mine] for a in applied]
    drive = [motional[c][mine] - coupling * own[c] for c in range(3)]
    current = [conduct_own * drive[c] + coil[c][mine] for c in range(3)]
    loads = [
        current[1] * applied_own[2] - current[2] * applied_own[1],
        current[2] * applied_own[0] - current[0] * applied_own[2],
        current[0] * applied_own[1] - current[1] * applied_own[0],
        conduct_own * (drive[0] * drive[0] + drive[1] * drive[1] + drive[2] * drive[2]),
    ]
    loads = jnp.concatenate(loads, 0)
    middle = half * nz
    turn_ref[...] = jnp.transpose(jnp.concatenate([loads[:, :middle], loads[:, middle:]], 0))
    for z in range(nz):
        send_ref[z] = turn_ref[pl.ds(z, half, stride=nz), :]


def flow_kernel(last, *refs):
    vel_ref, heat_ref, turb_ref, mate_ref, cross_ref, recv_ref = refs[:6]
    if last:
        together_ref, vel_hbm, heat_hbm, turb_hbm, pot_hbm = refs[6:11]
        bordered_ref, loads_ref, vel_out, heat_out, turb_out, pot_out, flat_ref, sems = refs[11:]
    else:
        labels_ref, table_ref = refs[6:8]
        vel_out, heat_out, turb_out, send_ref, mate_out, cross_out = refs[8:14]
        bordered_ref, loads_ref, sums_ref = refs[14:]
    odd = lax.rem(lax.axis_index("slab"), 2)
    rows, wide = heat_ref.shape[1:]
    count, half, packed = recv_ref.shape
    chunk = packed // 8
    moves = []
    if last:
        nz = pot_out.shape[1]
        together = together_ref[...]
        stacked, lanes = together.shape
        ny = lanes // nz
        for y in range(ny):
            line = pltpu.roll(together, lanes - y * nz, 1) if y else together
            flat_ref[pl.ds(y, stacked, stride=ny), :] = line[:, :LANES]
        pot_out[...] = flat_ref[:, :nz]
        moves.append(pltpu.make_async_copy(pot_out, pot_hbm, sems.at[0]))
        moves[0].start()
    edge = jnp.zeros((8, wide), jnp.float32)
    for f in range(6):
        for plane in range(2):
            bordered_ref[f, plane, 0:8, :] = edge
            bordered_ref[f, plane, 8 + rows :, :] = edge
            if f < 3:
                block = vel_ref[f, plane]
            elif f == 3:
                block = heat_ref[plane]
            else:
                block = turb_ref[f - 4, plane]
            bordered_ref[f, plane, 8 : 8 + rows, :] = block
    stacked = []
    for f in range(4):
        for side in range(2):
            at = (side * 4 + f) * chunk
            stacked.append(
                jnp.concatenate([recv_ref[s, :, at : at + chunk] for s in range(count)], 1)
            )
    spread = exact_dot(jnp.concatenate(stacked, 0), pair_chooser(wide, 1.0, True))
    for t in range(wide // LANES):
        part = spread[:, t * LANES : (t + 1) * LANES]
        loads_ref[t, pl.ds(0, 2 * rows, stride=2), :] = part
        loads_ref[t, pl.ds(1, 2 * rows, stride=2), :] = part
    lane = lax.broadcasted_iota(jnp.int32, (8, wide), 1)
    first_lane, last_lane = lane == 0, lane == wide - 1
    for top in range(0, rows, 8):
        tile = slice(top, top + 8)
        for plane in range(2):
            center = [bordered_ref[f, plane, 8 + top : 16 + top, :] for f in range(6)]
            kinetic, dissip = center[4], center[5]
            eddy_visc = eddy_coeff * kinetic * kinetic / jnp.maximum(dissip, turb_floor)
            strain = jnp.zeros((8, wide), jnp.float32)
            for f in range(6):
                here = center[f]
                spot = slice(f * rows + top, f * rows + top + 8)
                mate, cross_side = mate_ref[spot, :], cross_ref[spot, :]
                other = bordered_ref[f, 1 - plane, 8 + top : 16 + top, :]
                if plane == 0:
                    z_minus, z_plus = jnp.where(odd == 0, cross_side, mate), other
                else:
                    z_minus, z_plus = other, jnp.where(odd == 0, mate, cross_side)
                y_minus = bordered_ref[f, plane, 7 + top : 15 + top, :]
                y_plus = bordered_ref[f, plane, 9 + top : 17 + top, :]
                x_minus = jnp.where(first_lane, 0.0, pltpu.roll(here, 1, 1))
                x_plus = jnp.where(last_lane, 0.0, pltpu.roll(here, wide - 1, 1))
                grad_z = 0.5 * (z_plus - z_minus)
                grad_y = 0.5 * (y_plus - y_minus)
                grad_x = 0.5 * (x_plus - x_minus)
                laplace = z_plus + z_minus + y_plus + y_minus + x_plus + x_minus - 6.0 * here
                transport = center[0] * grad_x + center[1] * grad_y + center[2] * grad_z
                if f < 3:
                    strain += grad_x * grad_x + grad_y * grad_y + grad_z * grad_z
                    diffuse = molecular + eddy_visc
                    source = jnp.concatenate(
                        [
                            loads_ref[t, f * rows + top : f * rows + top + 8, :]
                            for t in range(wide // LANES)
                        ],
                        1,
                    )
                elif f == 3:
                    diffuse = heat_diffuse + eddy_visc * (1.0 / 0.9)
                    source = jnp.concatenate(
                        [
                            loads_ref[t, f * rows + top : f * rows + top + 8, :]
                            for t in range(wide // LANES)
                        ],
                        1,
                    )
                elif f == 4:
                    produce = eddy_visc * strain
                    diffuse = molecular + eddy_visc
                    source = produce - dissip
                else:
                    diffuse = molecular + eddy_visc * (1.0 / 1.3)
                    source = (
                        (prod_coeff * produce - dissip_coeff * dissip)
                        * dissip
                        / jnp.maximum(kinetic, turb_floor)
                    )
                fresh = here + time_step * (diffuse * laplace - transport + source)
                if f < 3:
                    vel_out[f, plane, tile, :] = fresh
                elif f == 3:
                    heat_out[plane, tile, :] = fresh
                else:
                    turb_out[f - 4, plane, tile, :] = fresh
                if not last and f < 4:
                    part = jnp.exp(-thermal_gradient_factor * fresh) if f == 3 else fresh
                    spot = slice(f * rows + top, f * rows + top + 8)
                    for t in range(wide // LANES):
                        piece = part[:, t * LANES : (t + 1) * LANES]
                        sums_ref[t, spot, :] = piece if plane == 0 else sums_ref[t, spot, :] + piece
        if last and (top + 8) % (rows // 2) == 0:
            span = pl.ds(top + 8 - rows // 2, rows // 2)
            for a, b in (
                (vel_out.at[:, :, span], vel_hbm.at[:, :, span]),
                (heat_out.at[:, span], heat_hbm.at[:, span]),
                (turb_out.at[:, :, span], turb_hbm.at[:, :, span]),
            ):
                moves.append(pltpu.make_async_copy(a, b, sems.at[len(moves)]))
                moves[-1].start()
    if last:
        for move in moves:
            move.wait()
        return
    split_planes(odd, vel_out, heat_out, turb_out, mate_out, cross_out)
    pack_windows(sums_ref, labels_ref, table_ref, send_ref, HALO - SWEEPS)


def call(kernel, outs, scratch, name, spaces, grant, cost, *operands, out_space=pltpu.VMEM):
    vmem = pl.BlockSpec(memory_space=pltpu.VMEM)
    special = {"s": pl.BlockSpec(memory_space=pltpu.SMEM), "h": pl.BlockSpec(memory_space=pltpu.HBM)}
    return pl.pallas_call(
        kernel,
        out_shape=[jax.ShapeDtypeStruct(s, jnp.float32) for s in outs],
        in_specs=[special.get(spaces.get(i), vmem) for i in range(len(operands))],
        out_specs=[pl.BlockSpec(memory_space=out_space)] * len(outs),
        scratch_shapes=[pltpu.VMEM(s, jnp.float32) if isinstance(s, tuple) else s for s in scratch],
        name=name,
        cost_estimate=pl.CostEstimate(flops=cost, bytes_accessed=cost, transcendentals=0),
        compiler_params=pltpu.CompilerParams(vmem_limit_bytes=grant << 20),
    )(*operands)


def beside(block):
    count = lax.axis_size("slab")
    mates = [(i, i ^ 1) for i in range(count)]
    across = [(i, i + 1) for i in range(1, count - 1, 2)]
    across = across + [(b, a) for a, b in across]
    return mates, across


def window_plan(
    melt_speeds,
    heat_state,
    eddy_quantities,
    zone_labels,
    zone_resistivity_inverse,
    imposed_induction,
    winding_current,
    window_entry_induction_guess,
):
    count = lax.axis_size("slab")
    _, chunk, ny, nz = imposed_induction.shape
    _, rows, wide = heat_state.shape
    mates, across = beside(None)
    flat = [
        a.reshape(3 * chunk * ny, nz)
        for a in (window_entry_induction_guess, imposed_induction, winding_current)
    ]
    window, narrow = chunk + 2 * HALO, chunk + 2 * (HALO - SWEEPS)
    tall = ny + ny // 2 if 4 * window > LANES else ny
    edge = (6 * rows, wide)
    joint = (6 * rows + 5 * chunk, wide)
    sums = (wide // LANES, 4 * rows, LANES)
    fields = (melt_speeds, heat_state, eddy_quantities)
    shapes = [a.shape for a in fields]
    fields = [pltpu.with_memory_space_constraint(a, pltpu.HBM) for a in fields]
    flat = [pltpu.with_memory_space_constraint(a, pltpu.HBM) for a in flat]
    mate, cross_side, *fields = call(
        edge_kernel,
        [joint, joint, *shapes],
        [(3 * chunk * ny, LANES), (3, 3 * chunk * ny, nz), pltpu.SemaphoreType.DMA((6,))],
        "edges",
        {i: "h" for i in range(6)},
        8,
        1 << 20,
        *fields,
        *flat,
    )
    block = mate
    mate = lax.ppermute(mate, "slab", mates)
    cross_side = lax.ppermute(cross_side, "slab", across)
    block_mate, block_cross = mate, cross_side
    (send,) = call(
        open_kernel,
        [(count, tall, LANES)],
        [sums],
        "open_windows",
        {3: "s"},
        8,
        1 << 22,
        fields[0],
        fields[1],
        zone_labels,
        zone_resistivity_inverse,
    )
    packed = (nz, ny // 2, 8 * chunk)
    for step_index in range(STEPS):
        first, last = step_index == 0, step_index == STEPS - 1
        arrived = lax.all_to_all(send, "slab", 0, 0, tiled=True)
        if not first:
            arrived, mate, cross_side = lax.optimization_barrier((arrived, mate, cross_side))
            mate = lax.ppermute(mate, "slab", mates)
            cross_side = lax.ppermute(cross_side, "slab", across)
        kept = () if first else (potential,)
        potential, loads = call(
            functools.partial(solve_kernel, chunk, ny, nz, rows, first),
            [(3 * (narrow if first else chunk), ny * nz), packed],
            [(2 if first else 1, ny * nz, LANES), (nz * ny // 2, LANES)],
            "sweeps",
            {},
            8,
            1 << 22,
            arrived,
            block,
            block_mate,
            block_cross,
            *kept,
        )
        loads = lax.all_to_all(loads, "slab", 0, 0, tiled=True)
        scratch = [(6, 2, rows + 16, wide), sums]
        if last:
            fields = call(
                functools.partial(flow_kernel, True),
                [*shapes, flat[0].shape],
                [*scratch, *shapes, flat[0].shape]
                + [(3 * chunk * ny, LANES), pltpu.SemaphoreType.DMA((7,))],
                "flow_last",
                {},
                12,
                1 << 22,
                *fields,
                mate,
                cross_side,
                loads,
                potential,
                out_space=pltpu.HBM,
            )
        else:
            *fields, send, mate, cross_side = call(
                functools.partial(flow_kernel, False),
                shapes + [(count, ny, LANES), edge, edge],
                scratch + [sums],
                "flow_first",
                {7: "s"},
                12,
                1 << 22,
                *fields,
                mate,
                cross_side,
                loads,
                zone_labels,
                zone_resistivity_inverse,
            )
    *fields, potential = fields
    return (*fields, potential.reshape(imposed_induction.shape))


def on_device(*arrays):
    count = lax.axis_size("slab")
    _, chunk, ny, nz = arrays[5].shape
    planes, rows, wide = arrays[1].shape
    narrow = chunk + 2 * (HALO - SWEEPS)
    fits = (
        STEPS == 2
        and planes == 2
        and nz == count
        and count % 2 == 0
        and chunk >= HALO
        and chunk % 8 == 0
        and ny % 16 == 0
        and 4 * narrow == LANES
        and 8 * chunk == LANES
        and nz * ny == 2 * LANES
        and wide == 2 * ny * nz
    )
    return window_plan(*arrays) if fits else per_sweep_plan(*arrays)


def solution(mesh):
    return jax.shard_map(
        on_device,
        mesh=mesh,
        in_specs=(
            P(None, ("groups", "slab"), None, None),
            P(("groups", "slab"), None, None),
            P(None, ("groups", "slab"), None, None),
            P(("groups", "slab"), None, None),
            P(),
            P(None, ("groups", "slab"), None, None),
            P(None, ("groups", "slab"), None, None),
            P(None, ("groups", "slab"), None, None),
        ),
        out_specs=(
            P(None, ("groups", "slab"), None, None),
            P(("groups", "slab"), None, None),
            P(None, ("groups", "slab"), None, None),
            P(None, ("groups", "slab"), None, None),
        ),
        check_vma=False,
    )
```

```python
import functools

import jax
import jax.numpy as jnp
from jax import lax
from jax.experimental import pallas as pl
from jax.experimental.pallas import tpu as pltpu
from jax.sharding import PartitionSpec as P


STEPS = 2
SWEEPS = 8


time_step = 0.02
molecular = 0.01
heat_diffuse = 0.01
eddy_coeff = 0.09
prod_coeff = 1.44
dissip_coeff = 1.92
turb_floor = 0.05
coupling = 1.0
thermal_gradient_factor = 0.3


def extended(block, sides, width):
    for axis, dim in sides:
        count = lax.axis_size(axis)
        forward = [(i, i + 1) for i in range(count - 1)]
        backward = [(target, source) for source, target in forward]
        low = lax.ppermute(
            lax.slice_in_dim(block, block.shape[dim] - width, None, axis=dim), axis, forward
        )
        high = lax.ppermute(lax.slice_in_dim(block, 0, width, axis=dim), axis, backward)
        block = jnp.concatenate([low, block, high], axis=dim)
    return block


def reduce_onto_parent(block):
    comps, depth, rows, cols = block.shape
    shaped = block.reshape(comps, depth // 2, 2, rows // 2, 2, cols // 2, 2)
    return jnp.mean(shaped, axis=(2, 4, 6))


def prolong(block):
    comps, depth, rows, cols = block.shape
    wide = jnp.broadcast_to(
        block[:, :, None, :, None, :, None], (comps, depth, 2, rows, 2, cols, 2)
    )
    return wide.reshape(comps, depth * 2, rows * 2, cols * 2)


def cross(left_vec, right_vec):
    return jnp.stack(
        [
            left_vec[1] * right_vec[2] - left_vec[2] * right_vec[1],
            left_vec[2] * right_vec[0] - left_vec[0] * right_vec[2],
            left_vec[0] * right_vec[1] - left_vec[1] * right_vec[0],
        ],
        0,
    )


def neighbours(padded):
    return (
        padded[:, 2:, 1:-1, 1:-1]
        + padded[:, :-2, 1:-1, 1:-1]
        + padded[:, 1:-1, 2:, 1:-1]
        + padded[:, 1:-1, :-2, 1:-1]
        + padded[:, 1:-1, 1:-1, 2:]
        + padded[:, 1:-1, 1:-1, :-2]
    )


def ohmic_admittance(zone_labels, zone_resistivity_inverse, heat_state):
    labels = jnp.arange(zone_resistivity_inverse.shape[0], dtype=jnp.int32)
    onehot = zone_labels[None] == labels[:, None, None, None]
    searched_higher = jnp.sum(
        jnp.where(onehot, zone_resistivity_inverse[:, None, None, None], jnp.float32(0.0)), axis=0
    )
    return (
        searched_higher
        * reduce_onto_parent(jnp.exp(-thermal_gradient_factor * heat_state)[None])[0]
    )


def faces(potential):
    padded = extended(potential, (("slab", 1),), 1)
    return jnp.pad(padded, ((0, 0), (0, 0), (1, 1), (1, 1)))


def relax(coupled, imposed_induction, winding_current, potential):
    conduct = coupled[3]
    motional = cross(coupled[:3], imposed_induction)
    source = conduct * motional + winding_current
    diagonal = 6.0 + coupling * conduct
    for _ in range(SWEEPS):
        potential = (source + neighbours(faces(potential))) / diagonal
    drive_field = motional - coupling * potential
    current = conduct * drive_field + winding_current
    lorentz = cross(current, imposed_induction)
    joule = conduct * jnp.sum(drive_field * drive_field, axis=0)
    return (potential, jnp.concatenate([lorentz, joule[None]], 0))


def advance(padded, lorentz, joule):
    bordered = jnp.pad(padded, ((0, 0), (0, 0), (0, 0), (1, 1)))
    center = bordered[:, 1:-1, 1:-1, 1:-1]
    z_plus = bordered[:, 2:, 1:-1, 1:-1]
    z_minus = bordered[:, :-2, 1:-1, 1:-1]
    y_plus = bordered[:, 1:-1, 2:, 1:-1]
    y_minus = bordered[:, 1:-1, :-2, 1:-1]
    x_plus = bordered[:, 1:-1, 1:-1, 2:]
    x_minus = bordered[:, 1:-1, 1:-1, :-2]
    grad_z = 0.5 * (z_plus - z_minus)
    grad_y = 0.5 * (y_plus - y_minus)
    grad_x = 0.5 * (x_plus - x_minus)
    laplace = z_plus + z_minus + y_plus + y_minus + x_plus + x_minus - 6.0 * center
    kinetic = center[4]
    dissip = center[5]
    transport = center[0] * grad_x + center[1] * grad_y + center[2] * grad_z
    eddy_visc = eddy_coeff * kinetic * kinetic / jnp.maximum(dissip, turb_floor)
    strain = jnp.sum(
        grad_x[:3] * grad_x[:3] + grad_y[:3] * grad_y[:3] + grad_z[:3] * grad_z[:3], axis=0
    )
    produce = eddy_visc * strain
    diffuse = jnp.stack(
        [
            molecular + eddy_visc,
            molecular + eddy_visc,
            molecular + eddy_visc,
            heat_diffuse + eddy_visc / 0.9,
            molecular + eddy_visc,
            molecular + eddy_visc / 1.3,
        ],
        0,
    )
    dissip_source = (
        (prod_coeff * produce - dissip_coeff * dissip) * dissip / jnp.maximum(kinetic, turb_floor)
    )
    source = jnp.concatenate(
        [lorentz, joule[None], (produce - dissip)[None], dissip_source[None]], 0
    )
    return center + time_step * (diffuse * laplace - transport + source)


def flow_step(induction_tables, em_loads):
    padded = extended(induction_tables, (("slab", 1),), 1)
    padded = jnp.pad(padded, ((0, 0), (0, 0), (1, 1), (0, 0)))
    return advance(padded, em_loads[:3], em_loads[3])


def local_coupled(induction_tables, zone_labels, zone_resistivity_inverse):
    conduct = ohmic_admittance(zone_labels, zone_resistivity_inverse, induction_tables[3])
    return jnp.concatenate([reduce_onto_parent(induction_tables[:3]), conduct[None]], 0)


def per_sweep_plan(
    melt_speeds,
    heat_state,
    eddy_quantities,
    zone_labels,
    zone_resistivity_inverse,
    imposed_induction,
    winding_current,
    window_entry_induction_guess,
):
    induction_tables = jnp.concatenate([melt_speeds, heat_state[None], eddy_quantities], 0)
    arrived = (
        lax.all_to_all(
            window_entry_induction_guess, "slab", split_axis=3, concat_axis=1, tiled=True
        ),
        lax.all_to_all(imposed_induction, "slab", split_axis=3, concat_axis=1, tiled=True),
        lax.all_to_all(winding_current, "slab", split_axis=3, concat_axis=1, tiled=True),
    )
    potential = jnp.transpose(arrived[0], (0, 3, 2, 1))
    field_local = jnp.transpose(arrived[1], (0, 3, 2, 1))
    coil_local = jnp.transpose(arrived[2], (0, 3, 2, 1))
    for _ in range(STEPS):
        coupled = local_coupled(induction_tables, zone_labels, zone_resistivity_inverse)
        potential, em_loads = relax(coupled, field_local, coil_local, potential)
        induction_tables = flow_step(induction_tables, prolong(em_loads))
    potential = lax.all_to_all(
        jnp.transpose(potential, (0, 3, 2, 1)), "slab", split_axis=1, concat_axis=3, tiled=True
    )
    return (induction_tables[:3], induction_tables[3], induction_tables[4:], potential)


HALO = 2 * SWEEPS
LANES = 128


def exact_dot(values, chooser):
    high = values.astype(jnp.bfloat16)
    rest = values - high.astype(jnp.float32)
    middle = rest.astype(jnp.bfloat16)
    low = (rest - middle.astype(jnp.float32)).astype(jnp.bfloat16)
    rows = values.shape[0]
    parts = jnp.dot(
        jnp.concatenate([high, middle, low], 0), chooser, preferred_element_type=jnp.float32
    )
    return parts[:rows] + (parts[rows : 2 * rows] + parts[2 * rows :])


def pair_chooser(wide, weight, transposed):
    shape = (wide // 2, wide) if transposed else (wide, wide // 2)
    fine = lax.broadcasted_iota(jnp.int32, shape, 1 if transposed else 0)
    coarse = lax.broadcasted_iota(jnp.int32, shape, 0 if transposed else 1)
    picked = lax.shift_right_logical(fine, 1) == coarse
    return jnp.where(picked, jnp.float32(weight), jnp.float32(0.0)).astype(jnp.bfloat16)


def pack_windows(sums_ref, admit_ref, send_ref, halo):
    tiles, rows, _ = sums_ref.shape
    wide = tiles * LANES
    count, ny = send_ref.shape[0], admit_ref.shape[0]
    paired = jnp.concatenate(
        [
            sums_ref[t, pl.ds(0, rows // 2, stride=2), :] + sums_ref[t, pl.ds(1, rows // 2, stride=2), :]
            for t in range(tiles)
        ],
        1,
    )
    coarse = exact_dot(paired, pair_chooser(wide, 0.125, False))
    coupled = jnp.concatenate([coarse[: 3 * ny], coarse[3 * ny :] * admit_ref[...]], 0)
    nx = wide // 2
    chunk = nx // count
    window = chunk + 2 * halo
    padded = jnp.concatenate([coupled, jnp.zeros((4 * ny, LANES), jnp.float32)], 1)
    padded = pltpu.roll(padded, halo, 1)
    for target in range(count):
        start = target * chunk
        joined = jnp.concatenate(
            [padded[f * ny : (f + 1) * ny, start : start + window] for f in range(4)], 1
        )
        send_ref[target, :ny, :] = joined[:, :LANES]
        if 4 * window > LANES:
            half = ny // 2
            send_ref[target, ny:, :] = jnp.concatenate(
                [joined[:half, LANES:], joined[half:, LANES:]], 1
            )


def edge_kernel(
    vel_ref,
    heat_ref,
    turb_ref,
    guess_ref,
    applied_ref,
    coil_ref,
    labels_ref,
    table_ref,
    block_ref,
    mate_ref,
    cross_ref,
    admit_ref,
    vel_out,
    heat_out,
    turb_out,
    flat_ref,
    raw_ref,
    zones_ref,
    known_ref,
    sems,
):
    odd = lax.rem(lax.axis_index("slab"), 2)
    pairs = [(guess_ref, raw_ref.at[0]), (applied_ref, raw_ref.at[1]), (coil_ref, raw_ref.at[2])]
    pairs += [(vel_ref, vel_out), (heat_ref, heat_out), (turb_ref, turb_out)]
    pairs += [(labels_ref, zones_ref), (table_ref, known_ref)]
    moves = [pltpu.make_async_copy(a, b, sems.at[i]) for i, (a, b) in enumerate(pairs)]
    for move in moves:
        move.start()
    for move in moves[:3]:
        move.wait()
    total, nz = guess_ref.shape
    chunk = block_ref.shape[0] // 5
    ny = total // (3 * chunk)
    lanes = ny * nz
    for kind in range(3):
        flat_ref[:, kind * nz : (kind + 1) * nz] = raw_ref[kind]
    lines = [flat_ref[pl.ds(y, 3 * chunk, stride=ny), :] for y in range(ny)]
    for kind in range(3):
        packed = jnp.concatenate([line[:, kind * nz : (kind + 1) * nz] for line in lines], 1)
        for c in range(3):
            block_ref[block_spot(3 * kind + c, chunk, lanes)] = packed[c * chunk : (c + 1) * chunk]
    for move in moves[3:]:
        move.wait()
    split_planes(odd, vel_out, heat_out, turb_out, mate_ref, cross_ref)
    labels = zones_ref[0]
    admittance = jnp.zeros(labels.shape, jnp.float32)
    for region in range(table_ref.shape[0]):
        admittance = jnp.where(labels == region, known_ref[region], admittance)
    admit_ref[...] = admittance


def split_planes(odd, vel_ref, heat_ref, turb_ref, mate_ref, cross_ref):
    rows = heat_ref.shape[1]
    for f in range(6):
        spot = slice(f * rows, (f + 1) * rows)
        for ref, plane in ((mate_ref, 1 - odd), (cross_ref, odd)):
            if f < 3:
                ref[spot, :] = vel_ref[f, plane]
            elif f == 3:
                ref[spot, :] = heat_ref[plane]
            else:
                ref[spot, :] = turb_ref[f - 4, plane]


def block_spot(index, chunk, lanes):
    row, lane = index % 5 * chunk, index // 5 * lanes
    return slice(row, row + chunk), slice(lane, lane + lanes)


def open_kernel(vel_ref, heat_ref, admit_ref, send_ref, sums_ref):
    rows = heat_ref.shape[1]
    for t in range(sums_ref.shape[0]):
        at = slice(t * LANES, (t + 1) * LANES)
        for c in range(3):
            sums_ref[t, c * rows : (c + 1) * rows, :] = vel_ref[c, 0, :, at] + vel_ref[c, 1, :, at]
        sums_ref[t, 3 * rows :, :] = jnp.exp(
            -thermal_gradient_factor * heat_ref[0, :, at]
        ) + jnp.exp(-thermal_gradient_factor * heat_ref[1, :, at])
    pack_windows(sums_ref, admit_ref, send_ref, HALO)


def solve_kernel(chunk, ny, nz, first, *refs):
    if first:
        recv_ref, block_ref, mate_ref, cross_ref, kept_ref, send_ref, wide_ref, turn_ref = refs
        halo = HALO
    else:
        recv_ref, held_ref, pot_out, send_ref, wide_ref, turn_ref = refs
        halo = HALO - SWEEPS
    window = chunk + 2 * halo
    place = lax.axis_index("slab")
    count = lax.axis_size("slab")
    odd = lax.rem(place, 2)
    half = ny // 2
    for z in range(nz):
        wide_ref[0, pl.ds(z, ny, stride=nz), :] = recv_ref[z, :ny, :]
        if 4 * window > LANES:
            tail = recv_ref[z, ny:, :]
            wide_ref[1, pl.ds(z, half, stride=nz), :] = tail
            wide_ref[1, pl.ds(half * nz + z, half, stride=nz), :] = pltpu.roll(tail, LANES // 2, 1)
    turned = jnp.concatenate([jnp.transpose(wide_ref[t]) for t in range(wide_ref.shape[0])], 0)
    velocity = [turned[c * window : (c + 1) * window] for c in range(3)]
    conduct = turned[3 * window : 4 * window]

    def windowed(kind):
        found = []
        for c in range(3):
            if not first:
                at = (3 * kind + c) * window
                found.append(held_ref[at : at + window, :])
                continue
            spot = block_spot(3 * kind + c, chunk, ny * nz)
            mate, cross_side = mate_ref[spot], cross_ref[spot]
            low = jnp.where(odd == 0, cross_side, mate)
            high = jnp.where(odd == 0, mate, cross_side)
            found.append(
                jnp.concatenate(
                    [low[chunk - halo :], block_ref[spot], high[:halo]], 0
                )
            )
        return found

    applied, coil = windowed(1), windowed(2)
    potential = jnp.concatenate(windowed(0), 0)
    motional = [
        velocity[1] * applied[2] - velocity[2] * applied[1],
        velocity[2] * applied[0] - velocity[0] * applied[2],
        velocity[0] * applied[1] - velocity[1] * applied[0],
    ]
    where_x = place * chunk - halo + lax.broadcasted_iota(jnp.int32, (window, ny * nz), 0)
    inside = (where_x >= 0) & (where_x < count * chunk)
    inverse = jnp.where(inside, 1.0 / (6.0 + coupling * conduct), 0.0)
    source = jnp.concatenate([conduct * motional[c] + coil[c] for c in range(3)], 0)
    inverse = jnp.concatenate([inverse] * 3, 0)
    source = source * inverse
    shape = potential.shape
    lane = lax.broadcasted_iota(jnp.int32, shape, 1)
    column = lax.rem(lane, nz)
    for _ in range(SWEEPS):
        around = pltpu.roll(potential, 1, 0) + pltpu.roll(potential, shape[0] - 1, 0)
        around += jnp.where(column == 0, 0.0, pltpu.roll(potential, 1, 1))
        around += jnp.where(column == nz - 1, 0.0, pltpu.roll(potential, shape[1] - 1, 1))
        around += jnp.where(lane < nz, 0.0, pltpu.roll(potential, nz, 1))
        around += jnp.where(lane >= shape[1] - nz, 0.0, pltpu.roll(potential, shape[1] - nz, 1))
        potential = source + around * inverse
    own = [potential[c * window + halo : c * window + halo + chunk] for c in range(3)]
    if first:
        keep = chunk + 2 * (halo - SWEEPS)
        whole = [potential[c * window : (c + 1) * window] for c in range(3)] + applied + coil
        for i, array in enumerate(whole):
            kept_ref[i * keep : (i + 1) * keep, :] = array[SWEEPS : SWEEPS + keep]
    else:
        pot_out[...] = jnp.concatenate(own, 0)
    mine = slice(halo, halo + chunk)
    conduct_own = conduct[mine]
    applied_own = [a[mine] for a in applied]
    drive = [motional[c][mine] - coupling * own[c] for c in range(3)]
    current = [conduct_own * drive[c] + coil[c][mine] for c in range(3)]
    loads = [
        current[1] * applied_own[2] - current[2] * applied_own[1],
        current[2] * applied_own[0] - current[0] * applied_own[2],
        current[0] * applied_own[1] - current[1] * applied_own[0],
        conduct_own * (drive[0] * drive[0] + drive[1] * drive[1] + drive[2] * drive[2]),
    ]
    loads = jnp.concatenate(loads, 0)
    middle = half * nz
    turn_ref[...] = jnp.transpose(jnp.concatenate([loads[:, :middle], loads[:, middle:]], 0))
    for z in range(nz):
        send_ref[z] = turn_ref[pl.ds(z, half, stride=nz), :]


def flow_kernel(last, *refs):
    vel_ref, heat_ref, turb_ref, mate_ref, cross_ref, recv_ref = refs[:6]
    if last:
        together_ref, vel_hbm, heat_hbm, turb_hbm, pot_hbm = refs[6:11]
        bordered_ref, loads_ref, vel_out, heat_out, turb_out, pot_out, flat_ref, sems = refs[11:]
    else:
        admit_ref = refs[6]
        vel_out, heat_out, turb_out, send_ref, mate_out, cross_out = refs[7:13]
        bordered_ref, loads_ref, sums_ref = refs[13:]
    odd = lax.rem(lax.axis_index("slab"), 2)
    rows, wide = heat_ref.shape[1:]
    count, _, packed = recv_ref.shape
    chunk = packed // 8
    moves = []
    if last:
        nz = pot_out.shape[1]
        together = together_ref[...]
        stacked, lanes = together.shape
        ny = lanes // nz
        for y in range(ny):
            line = pltpu.roll(together, lanes - y * nz, 1) if y else together
            flat_ref[pl.ds(y, stacked, stride=ny), :] = line[:, :LANES]
        pot_out[...] = flat_ref[:, :nz]
        moves.append(pltpu.make_async_copy(pot_out, pot_hbm, sems.at[0]))
        moves[0].start()
    edge = jnp.zeros((8, wide), jnp.float32)
    for f in range(6):
        for plane in range(2):
            bordered_ref[f, plane, 0:8, :] = edge
            bordered_ref[f, plane, 8 + rows :, :] = edge
            if f < 3:
                block = vel_ref[f, plane]
            elif f == 3:
                block = heat_ref[plane]
            else:
                block = turb_ref[f - 4, plane]
            bordered_ref[f, plane, 8 : 8 + rows, :] = block
    stacked = []
    for f in range(4):
        for side in range(2):
            at = (side * 4 + f) * chunk
            stacked.append(
                jnp.concatenate([recv_ref[s, :, at : at + chunk] for s in range(count)], 1)
            )
    spread = exact_dot(jnp.concatenate(stacked, 0), pair_chooser(wide, 1.0, True))
    for t in range(wide // LANES):
        part = spread[:, t * LANES : (t + 1) * LANES]
        loads_ref[t, pl.ds(0, 2 * rows, stride=2), :] = part
        loads_ref[t, pl.ds(1, 2 * rows, stride=2), :] = part
    lane = lax.broadcasted_iota(jnp.int32, (8, wide), 1)
    first_lane, last_lane = lane == 0, lane == wide - 1
    for top in range(0, rows, 8):
        tile = slice(top, top + 8)
        for plane in range(2):
            center = [bordered_ref[f, plane, 8 + top : 16 + top, :] for f in range(6)]
            kinetic, dissip = center[4], center[5]
            eddy_visc = eddy_coeff * kinetic * kinetic / jnp.maximum(dissip, turb_floor)
            strain = jnp.zeros((8, wide), jnp.float32)
            for f in range(6):
                here = center[f]
                spot = slice(f * rows + top, f * rows + top + 8)
                mate, cross_side = mate_ref[spot, :], cross_ref[spot, :]
                other = bordered_ref[f, 1 - plane, 8 + top : 16 + top, :]
                if plane == 0:
                    z_minus, z_plus = jnp.where(odd == 0, cross_side, mate), other
                else:
                    z_minus, z_plus = other, jnp.where(odd == 0, mate, cross_side)
                y_minus = bordered_ref[f, plane, 7 + top : 15 + top, :]
                y_plus = bordered_ref[f, plane, 9 + top : 17 + top, :]
                x_minus = jnp.where(first_lane, 0.0, pltpu.roll(here, 1, 1))
                x_plus = jnp.where(last_lane, 0.0, pltpu.roll(here, wide - 1, 1))
                grad_z = 0.5 * (z_plus - z_minus)
                grad_y = 0.5 * (y_plus - y_minus)
                grad_x = 0.5 * (x_plus - x_minus)
                laplace = z_plus + z_minus + y_plus + y_minus + x_plus + x_minus - 6.0 * here
                transport = center[0] * grad_x + center[1] * grad_y + center[2] * grad_z
                if f < 3:
                    strain += grad_x * grad_x + grad_y * grad_y + grad_z * grad_z
                    diffuse = molecular + eddy_visc
                    source = jnp.concatenate(
                        [
                            loads_ref[t, f * rows + top : f * rows + top + 8, :]
                            for t in range(wide // LANES)
                        ],
                        1,
                    )
                elif f == 3:
                    diffuse = heat_diffuse + eddy_visc * (1.0 / 0.9)
                    source = jnp.concatenate(
                        [
                            loads_ref[t, f * rows + top : f * rows + top + 8, :]
                            for t in range(wide // LANES)
                        ],
                        1,
                    )
                elif f == 4:
                    produce = eddy_visc * strain
                    diffuse = molecular + eddy_visc
                    source = produce - dissip
                else:
                    diffuse = molecular + eddy_visc * (1.0 / 1.3)
                    source = (
                        (prod_coeff * produce - dissip_coeff * dissip)
                        * dissip
                        / jnp.maximum(kinetic, turb_floor)
                    )
                fresh = here + time_step * (diffuse * laplace - transport + source)
                if f < 3:
                    vel_out[f, plane, tile, :] = fresh
                elif f == 3:
                    heat_out[plane, tile, :] = fresh
                else:
                    turb_out[f - 4, plane, tile, :] = fresh
                if not last and f < 4:
                    part = jnp.exp(-thermal_gradient_factor * fresh) if f == 3 else fresh
                    spot = slice(f * rows + top, f * rows + top + 8)
                    for t in range(wide // LANES):
                        piece = part[:, t * LANES : (t + 1) * LANES]
                        sums_ref[t, spot, :] = piece if plane == 0 else sums_ref[t, spot, :] + piece
        if last and (top + 8) % (rows // 2) == 0:
            span = pl.ds(top + 8 - rows // 2, rows // 2)
            for a, b in (
                (vel_out.at[:, :, span], vel_hbm.at[:, :, span]),
                (heat_out.at[:, span], heat_hbm.at[:, span]),
                (turb_out.at[:, :, span], turb_hbm.at[:, :, span]),
            ):
                moves.append(pltpu.make_async_copy(a, b, sems.at[len(moves)]))
                moves[-1].start()
    if last:
        for move in moves:
            move.wait()
        return
    split_planes(odd, vel_out, heat_out, turb_out, mate_out, cross_out)
    pack_windows(sums_ref, admit_ref, send_ref, HALO - SWEEPS)


def call(kernel, outs, scratch, spaces, grant, cost, *operands, out_space=None):
    vmem = pl.BlockSpec(memory_space=pltpu.VMEM)
    special = {"s": pl.BlockSpec(memory_space=pltpu.SMEM), "h": pl.BlockSpec(memory_space=pltpu.HBM)}
    return pl.pallas_call(
        kernel,
        out_shape=[jax.ShapeDtypeStruct(s, jnp.float32) for s in outs],
        in_specs=[special.get(spaces.get(i), vmem) for i in range(len(operands))],
        out_specs=[pl.BlockSpec(memory_space=m) for m in out_space or [pltpu.VMEM] * len(outs)],
        scratch_shapes=[pltpu.VMEM(s, jnp.float32) if isinstance(s, tuple) else s for s in scratch],
        cost_estimate=pl.CostEstimate(flops=cost, bytes_accessed=cost, transcendentals=0),
        compiler_params=pltpu.CompilerParams(vmem_limit_bytes=grant << 20),
    )(*operands)


def trade(mate, cross_side):
    count = lax.axis_size("slab")
    mates = [(i, i ^ 1) for i in range(count)]
    across = [(i, i + 1) for i in range(1, count - 1, 2)]
    across = across + [(b, a) for a, b in across]
    cross_side = lax.ppermute(cross_side, "slab", across)
    mate = lax.ppermute(mate, "slab", mates)
    return mate, cross_side


def window_plan(
    melt_speeds,
    heat_state,
    eddy_quantities,
    zone_labels,
    zone_resistivity_inverse,
    imposed_induction,
    winding_current,
    window_entry_induction_guess,
):
    count = lax.axis_size("slab")
    _, chunk, ny, nz = imposed_induction.shape
    _, rows, wide = heat_state.shape
    flat = [
        a.reshape(3 * chunk * ny, nz)
        for a in (window_entry_induction_guess, imposed_induction, winding_current)
    ]
    window, narrow = chunk + 2 * HALO, chunk + 2 * (HALO - SWEEPS)
    tall = ny + ny // 2 if 4 * window > LANES else ny
    edge = (6 * rows, wide)
    sums = (wide // LANES, 4 * rows, LANES)
    fields = (melt_speeds, heat_state, eddy_quantities)
    shapes = [a.shape for a in fields]
    raw = [*fields, *flat, zone_labels, zone_resistivity_inverse]
    raw = [pltpu.with_memory_space_constraint(a, pltpu.HBM) for a in raw]
    block, mate, cross_side, admittance, *fields = call(
        edge_kernel,
        [(5 * chunk, wide), edge, edge, zone_labels.shape[1:], *shapes],
        [
            (3 * chunk * ny, LANES),
            (3, 3 * chunk * ny, nz),
            pltpu.VMEM(zone_labels.shape, jnp.int32),
            pltpu.SMEM(zone_resistivity_inverse.shape, jnp.float32),
            pltpu.SemaphoreType.DMA((len(raw),)),
        ],
        {i: "h" for i in range(len(raw))},
        8,
        1 << 20,
        *raw,
    )
    (send,) = call(
        open_kernel,
        [(count, tall, LANES)],
        [sums],
        {},
        8,
        1 << 22,
        fields[0],
        fields[1],
        admittance,
    )
    packed = (nz, ny // 2, 8 * chunk)
    for step_index in range(STEPS):
        first, last = step_index == 0, step_index == STEPS - 1
        arrived = lax.all_to_all(send, "slab", 0, 0, tiled=True)
        if first:
            held = (block, *trade(block, block))
        mate, cross_side = trade(mate, cross_side)
        potential, loads = call(
            functools.partial(solve_kernel, chunk, ny, nz, first),
            [(9 * narrow if first else 3 * chunk, ny * nz), packed],
            [(2 if first else 1, ny * nz, LANES), (nz * ny // 2, LANES)],
            {},
            8,
            1 << 22,
            arrived,
            *held,
        )
        held = (potential,)
        loads = lax.all_to_all(loads, "slab", 0, 0, tiled=True)
        scratch = [(6, 2, rows + 16, wide), sums]
        if last:
            fields = call(
                functools.partial(flow_kernel, True),
                [*shapes, flat[0].shape],
                [*scratch, *shapes, flat[0].shape]
                + [(3 * chunk * ny, LANES), pltpu.SemaphoreType.DMA((7,))],
                {},
                12,
                1 << 22,
                *fields,
                mate,
                cross_side,
                loads,
                potential,
                out_space=[pltpu.HBM] * 4,
            )
        else:
            *fields, send, mate, cross_side = call(
                functools.partial(flow_kernel, False),
                shapes + [(count, ny, LANES), edge, edge],
                scratch + [sums],
                {},
                12,
                1 << 22,
                *fields,
                mate,
                cross_side,
                loads,
                admittance,
            )
    *fields, potential = fields
    return (*fields, potential.reshape(imposed_induction.shape))


def on_device(*arrays):
    count = lax.axis_size("slab")
    _, chunk, ny, nz = arrays[5].shape
    planes, _, wide = arrays[1].shape
    narrow = chunk + 2 * (HALO - SWEEPS)
    fits = (
        STEPS == 2
        and planes == 2
        and nz == count
        and count % 2 == 0
        and chunk >= HALO
        and chunk % 8 == 0
        and ny % 16 == 0
        and 4 * narrow == LANES
        and 8 * chunk == LANES
        and nz * ny == 2 * LANES
        and wide == 2 * ny * nz
    )
    return window_plan(*arrays) if fits else per_sweep_plan(*arrays)


def solution(mesh):
    return jax.shard_map(
        on_device,
        mesh=mesh,
        in_specs=(
            P(None, ("groups", "slab"), None, None),
            P(("groups", "slab"), None, None),
            P(None, ("groups", "slab"), None, None),
            P(("groups", "slab"), None, None),
            P(),
            P(None, ("groups", "slab"), None, None),
            P(None, ("groups", "slab"), None, None),
            P(None, ("groups", "slab"), None, None),
        ),
        out_specs=(
            P(None, ("groups", "slab"), None, None),
            P(("groups", "slab"), None, None),
            P(None, ("groups", "slab"), None, None),
            P(None, ("groups", "slab"), None, None),
        ),
        check_vma=False,
    )
```
